256 devices in a mesh: dp: 4 (over x), expert: 64 (over y, z, core).
Axes of the slice: x: 4, y: 4, z: 8, core: 2. Of those that a mesh axis runs over, the one named last changes fastest.
Arguments:
- tokens: bfloat16 [32768, 2048], P(('dp', 'expert')), may hold values from -6 to 6
- cotangent: bfloat16 [32768, 2048], P(('dp', 'expert')), may hold values from -6 to 6
- gate_probs: bfloat16 [32768, 2], P(('dp', 'expert')), may hold values from 0.099609375 to 0.8984375
- expert_ids: int32 [32768, 2], P(('dp', 'expert')), may hold values from 0 to 127, all different within a row; in each aligned block of 128 rows (0 to 127, 128 to 255, ...) at most 3 rows name the same one
- gate_weight: bfloat16 [64, 2048, 768], P('expert'), may hold values from -0.125 to 0.125
- up_weight: bfloat16 [64, 2048, 768], P('expert'), may hold values from -0.125 to 0.125
- down_weight: bfloat16 [64, 768, 2048], P('expert'), may hold values from -0.21875 to 0.21875
Outputs:
- grad_tokens: bfloat16 [32768, 2048], P(('dp', 'expert'))
- grad_probs: bfloat16 [32768, 2], P(('dp', 'expert'))
- grad_gate: bfloat16 [64, 2048, 768], P('expert', 'dp')
- grad_up: bfloat16 [64, 2048, 768], P('expert', 'dp')
- grad_down: bfloat16 [64, 768, 2048], P('expert', None, 'dp')
The draws below stay inside these ranges and needn't reach their ends.
Inputs may be any that keep to these rules, and one draw needn't show every extreme that they name: `expert_ids`: each row names 2 different slots; among the 128 tokens of one device no slot is named more than 3 times, a bound that some block reaches.
All inputs are finite; a program needn't handle non-finite values.
Results may differ from the reference program's by a relative error of at most 0.009.
Values may be sent and summed in bfloat16 or wider, within the bound.
No kernel may reach another device: no remote copies, remote signals or barrier semaphores. Data moves between devices by JAX's collectives and lax.ppermute only.
A program may use at most 128 MiB of HBM per device.

```python
import math
import jax
import jax.numpy as jnp
import numpy as np
from jax import lax

D = 2048
FF = 768
TOPK = 2
TOK_DEV = 128
EXPERTS = 64
REPLICAS = 4
CAP = 3
TOKENS = 32768


def level_of(stream_key, extent, shards, smallest, top_value):
    def one(axis_at, parts):
        heights = jax.random.uniform(jax.random.fold_in(jax.random.fold_in(stream_key, 6), axis_at), (parts,), jnp.float32, smallest / len(shards), top_value / len(shards))
        return jnp.repeat(jnp.exp(heights), extent[axis_at] // parts).reshape((-1,) + (1,) * (len(extent) - axis_at - 1))

    gain = one(*shards[0])
    for cut in shards[1:]:
        gain = gain * one(*cut)
    return gain


def routed_block(key, own, number, rows, count, top, limit, slope):
    order = jax.random.permutation(key, count)
    crowded, usual = portions_of(count, rows * top, limit, slope, True), portions_of(count, rows * top, limit, slope, False)
    places = jnp.arange(count)

    def named(tallies, rotation):
        used = int((tallies > 0).sum())
        fixed = max(1, used // 4)
        moved = fixed + (places - fixed + rotation * (used - fixed)) % max(1, count - fixed)
        return jnp.zeros((count,), jnp.int32).at[order[jnp.where(places < fixed, places, moved)]].set(jnp.asarray(tallies, jnp.int32))

    tallies = jnp.where(number % 4 == 0, named(crowded, number // 4), named(usual, number - number // 4 - 1))
    mixed = jax.random.permutation(jax.random.fold_in(own, 3), count)
    source_of, taker = mixed[0:count // 2 * 2:2], mixed[1:count // 2 * 2:2]
    margin = jnp.minimum(tallies[source_of] - 1, limit - tallies[taker]) // 2
    margin = jnp.where((source_of == order[0]) | (taker == order[0]) | (tallies[taker] == 0), 0, jnp.maximum(margin, 0))
    moved = jax.random.randint(jax.random.fold_in(own, 4), (count // 2,), 0, 1 << 20) % (margin + 1)
    tallies = tallies.at[source_of].add(-moved).at[taker].add(moved)
    members = jnp.searchsorted(jnp.cumsum(tallies), jnp.arange(rows * top), side="right").astype(jnp.int32)
    grid = members.reshape(top, rows).T
    grid = grid[jax.random.permutation(jax.random.fold_in(own, 1), rows)]
    rotation = jax.random.randint(jax.random.fold_in(own, 2), (rows, 1), 0, top)
    return jnp.take_along_axis(grid, (jnp.arange(top)[None, :] + rotation) % top, axis=1)


def portions_of(number_of, total, reach, slope, full):
    loads = [(1 << 20) // math.isqrt(standing ** slope) + 1 for standing in range(1, number_of + 1)]
    largest = reach if full else min(reach, max(-(-total // number_of), total * loads[0] // sum(loads)))
    least = 1 if total - largest >= number_of - 1 else 0
    counts, surplus = [largest] + [least] * (number_of - 1), total - largest - least * (number_of - 1)
    while surplus > 0:
        candidates = [i for i in range(1, number_of) if counts[i] < largest] or [i for i in range(1, number_of) if counts[i] < reach]
        mass, left = sum([loads[i] for i in candidates]), surplus
        for i in candidates:
            more = min(reach - counts[i], max(1, left * loads[i] // mass), surplus)
            counts[i] = counts[i] + more
            surplus = surplus - more
    return np.array(counts)


def bell_draw(stream_key, extent, scale, reach, cuts=(), kind=jnp.bfloat16):
    result = jax.random.normal(stream_key, extent, jnp.float32) * scale
    if len(cuts) > 0:
        result = level_of(stream_key, extent, cuts, -0.22, 0.18) * result
    return jnp.clip(result, min=-reach, max=reach).astype(kind)


def setup_inputs(seed: int = 0) -> dict:
    splits = jax.random.split(jax.random.key(seed), 8)
    tokens = bell_draw(splits[0], (TOKENS, D), 1.0, 6.0, ((0, 256),))
    cotangent = bell_draw(splits[1], (TOKENS, D), 1.0, 6.0, ((0, 256),))
    gate_probs = jnp.clip(0.099609375 + 0.7988281 * jax.random.uniform(splits[2], (TOKENS, TOPK), jnp.float32) ** level_of(splits[2], (TOKENS, TOPK), ((0, 256),), -0.2, 0.2), 0.099609375, 0.8984375).astype(jnp.bfloat16)
    expert_ids_keys = jax.random.split(jax.random.fold_in(splits[3], 1), TOKENS // TOK_DEV)
    expert_ids_turns = jax.random.permutation(jax.random.fold_in(splits[3], 3), TOKENS // TOK_DEV)
    expert_ids = jax.vmap(lambda own, number: routed_block(jax.random.fold_in(splits[3], 2), own, number, TOK_DEV, 2 * EXPERTS, TOPK, CAP, 2))(expert_ids_keys, expert_ids_turns).reshape((TOKENS, TOPK))
    gate_weight = bell_draw(splits[4], (EXPERTS, D, FF), D ** -0.5, 0.125, ((0, 64),))
    up_weight = bell_draw(splits[5], (EXPERTS, D, FF), D ** -0.5, 0.125, ((0, 64),))
    down_weight = bell_draw(splits[6], (EXPERTS, FF, D), FF ** -0.5, 0.21875, ((0, 64),))
    return {"tokens": tokens, "cotangent": cotangent, "gate_probs": gate_probs, "expert_ids": expert_ids, "gate_weight": gate_weight, "up_weight": up_weight, "down_weight": down_weight}


def rounded(values):
    return lax.optimization_barrier(values.astype(jnp.bfloat16)).astype(jnp.float32)


def contract_last(left, right):
    return lax.dot_general(left, right, (((1,), (1,)), ((), ())), preferred_element_type=jnp.float32)


def expert_rows(inputs, cot_rows, prob_rows, gate_w, up_w, down_w):
    gate_pre = jnp.dot(inputs, gate_w, preferred_element_type=jnp.float32)
    up_pre = jnp.dot(inputs, up_w, preferred_element_type=jnp.float32)
    sigmoid_g = jax.nn.sigmoid(gate_pre)
    activated = gate_pre * sigmoid_g
    hidden = (activated * up_pre).astype(jnp.bfloat16)
    output = jnp.dot(hidden, down_w, preferred_element_type=jnp.float32)
    cot_float = cot_rows.astype(jnp.float32)
    prob_grad = jnp.sum(output * cot_float, axis=1).astype(jnp.bfloat16)
    scaled = (prob_rows.astype(jnp.float32)[:, None] * cot_float).astype(jnp.bfloat16)
    back_hidden = contract_last(scaled, down_w)
    back_gate = (back_hidden * up_pre * sigmoid_g * (1.0 + gate_pre * (1.0 - sigmoid_g))).astype(jnp.bfloat16)
    back_up = (back_hidden * activated).astype(jnp.bfloat16)
    back_rows = (contract_last(back_gate, gate_w) + contract_last(back_up, up_w)).astype(jnp.bfloat16)
    return back_rows, prob_grad, hidden, scaled, back_gate, back_up


def reference(tokens, cotangent, gate_probs, expert_ids, gate_weight, up_weight, down_weight):
    halfway = EXPERTS // 2
    routed = TOK_DEV * TOPK
    slot_rows = EXPERTS * CAP
    total = 2 * EXPERTS * slot_rows
    slot_ids = expert_ids.reshape(REPLICAS, EXPERTS, routed).astype(jnp.int32)
    columns = jnp.arange(2 * EXPERTS, dtype=jnp.int32)
    onehot = (slot_ids[..., None] == columns).astype(jnp.int32)
    ranking = jnp.sum((jnp.cumsum(onehot, axis=2) - onehot) * onehot, axis=3).astype(jnp.int32)
    senders = jnp.arange(EXPERTS, dtype=jnp.int32)[None, :, None]
    placed = ((slot_ids * EXPERTS + senders) * CAP + ranking).astype(jnp.int32)
    replica = jnp.broadcast_to(jnp.arange(REPLICAS, dtype=jnp.int32)[:, None, None], placed.shape)
    partner = jnp.bitwise_xor(jnp.arange(EXPERTS, dtype=jnp.int32), halfway)

    def arrange(values):
        empty = jnp.zeros((REPLICAS, total) + values.shape[3:], values.dtype)
        filled = empty.at[replica, placed].set(values)
        return filled.reshape((REPLICAS, 2 * EXPERTS, slot_rows) + values.shape[3:])

    def pair_up(buffer):
        stacked = jnp.stack([buffer[:, :EXPERTS], buffer[:, EXPERTS + partner]], axis=2)
        return jnp.moveaxis(stacked, 1, 0)

    def unpair(values):
        moved = jnp.moveaxis(values, 0, 2)
        whole = jnp.concatenate([moved[:, 0], moved[:, 1][:, partner]], axis=1)
        return whole.reshape((REPLICAS, total) + values.shape[4:])

    token_rows = jnp.repeat(tokens.reshape(REPLICAS, EXPERTS, TOK_DEV, D), TOPK, axis=2)
    cot_rows = jnp.repeat(cotangent.reshape(REPLICAS, EXPERTS, TOK_DEV, D), TOPK, axis=2)
    prob_rows = gate_probs.reshape(REPLICAS, EXPERTS, routed)

    def settle(partial_sums):
        per_slot = rounded(partial_sums).reshape((REPLICAS, 2) + partial_sums.shape[1:])
        per_pair = rounded(jnp.sum(per_slot, axis=1))
        return jnp.sum(per_pair, axis=0).astype(jnp.bfloat16)

    def per_expert(packed):
        inputs, cots, probs, gate_w, up_w, down_w = packed
        batch = REPLICAS * 2
        back_rows, prob_grad, hidden, scaled, back_gate, back_up = expert_rows(
            inputs.reshape(-1, D), cots.reshape(-1, D), probs.reshape(-1), gate_w, up_w, down_w)
        inputs_f = inputs.reshape(batch, slot_rows, D).astype(jnp.float32)
        gate_part = jnp.einsum("bmd,bmf->bdf", inputs_f, back_gate.reshape(batch, slot_rows, FF).astype(jnp.float32))
        up_part = jnp.einsum("bmd,bmf->bdf", inputs_f, back_up.reshape(batch, slot_rows, FF).astype(jnp.float32))
        down_part = jnp.einsum("bmf,bmd->bfd", hidden.reshape(batch, slot_rows, FF).astype(jnp.float32),
                               scaled.reshape(batch, slot_rows, D).astype(jnp.float32))
        return (back_rows.reshape(REPLICAS, 2, slot_rows, D), prob_grad.reshape(REPLICAS, 2, slot_rows),
                settle(gate_part), settle(up_part), settle(down_part))

    back_all, prob_all, grad_gate, grad_up, grad_down = lax.map(
        per_expert, (pair_up(arrange(token_rows)), pair_up(arrange(cot_rows)), pair_up(arrange(prob_rows)),
                     gate_weight, up_weight, down_weight))
    back = unpair(back_all)[replica, placed]
    grad_tokens = jnp.sum(back.reshape(REPLICAS, EXPERTS, TOK_DEV, TOPK, D).astype(jnp.float32), axis=3)
    grad_tokens = grad_tokens.astype(jnp.bfloat16).reshape(TOKENS, D)
    grad_probs = unpair(prob_all)[replica, placed].reshape(TOKENS, TOPK)
    return grad_tokens, grad_probs, grad_gate, grad_up, grad_down
```

```python
import jax
import jax.numpy as jnp
import numpy as np
from jax import lax
from jax.experimental import pallas as pl
from jax.experimental.pallas import tpu as pltpu
from jax.sharding import PartitionSpec as P

F32 = jnp.float32
BF16 = jnp.bfloat16
N = 64
CAP = 3
PER = 2 * CAP
ROWS = N * PER
D = 2048
FF = 768
TOK = 128
DP = 4
SEG = 512
NSEG = D // SEG
SPAN = NSEG * PER
BSEG = 256
NBSEG = D // BSEG
BSPAN = NBSEG * PER + 8
GROUP = 8
GROWS = GROUP * PER
NGROUP = N // GROUP
FB = 256
NFB = FF // FB


def permutations():
    unmix = np.zeros((NSEG * GROWS, GROUP * SPAN), np.float32)
    back = np.zeros((NBSEG * GROWS + 16, GROUP * BSPAN), np.float32)
    mark = np.zeros((GROWS, BSEG), np.float32)
    spread = np.zeros((GROUP * BSPAN, GROWS), np.float32)
    for d in range(GROUP):
        for j in range(PER):
            row = d * PER + j
            mark[row, j] = 1
            spread[d * BSPAN + NBSEG * PER, row] = 1
            for s in range(NSEG):
                unmix[s * GROWS + row, d * SPAN + s * PER + j] = 1
            for s in range(NBSEG):
                back[s * GROWS + row, d * BSPAN + s * PER + j] = 1
        back[NBSEG * GROWS + d, d * BSPAN + NBSEG * PER] = 1
    mix = np.concatenate([back[: NBSEG * GROWS].T, spread], axis=1)
    return unmix, back, mix, mark


UNMIX, BACK, MIX, MARK = permutations()


def mm(a, b):
    return jnp.dot(a, b, preferred_element_type=F32)


def mm_t(a, b):
    return lax.dot_general(a, b, (((1,), (1,)), ((), ())), preferred_element_type=F32)


def iota(shape, dim):
    return lax.broadcasted_iota(jnp.int32, shape, dim)


def split_slot(ids):
    is_copy = (ids >= N).astype(jnp.int32)
    base = ids - N * is_copy
    target = jnp.where(ids >= N, jnp.bitwise_xor(base, N // 2), base)
    return target, is_copy * CAP


def places_in_lanes(ids_ref):
    ids = [ids_ref[k : k + 1, :] for k in range(2)]
    hot = [(iota((2 * N, TOK), 0) == v).astype(F32) for v in ids]
    before = (iota((TOK, TOK), 0) < iota((TOK, TOK), 1)).astype(F32).astype(BF16)
    count = mm((hot[0] + hot[1]).astype(BF16), before)
    out = []
    for k in range(2):
        rank = jnp.sum(count * hot[k], axis=0, keepdims=True).astype(jnp.int32)
        target, first = split_slot(ids[k])
        out.append((target, first + rank))
    return out


def places_in_rows(ids_ref):
    ids = [ids_ref[:, k : k + 1] for k in range(2)]
    hot = [(iota((TOK, 2 * N), 1) == v).astype(F32) for v in ids]
    before = (iota((TOK, TOK), 1) < iota((TOK, TOK), 0)).astype(F32).astype(BF16)
    count = mm(before, (hot[0] + hot[1]).astype(BF16))
    out = []
    for k in range(2):
        rank = jnp.sum(count * hot[k], axis=1, keepdims=True).astype(jnp.int32)
        target, first = split_slot(ids[k])
        out.append((target, first + rank))
    return out


def send_rows(ids_ref, weights, x_ref, out_ref):
    lanes = []
    for target, slot in places_in_lanes(ids_ref):
        at = target * SPAN + slot
        lanes.append(jnp.concatenate([at + s * PER for s in range(NSEG)], axis=1))
    stacked = jnp.concatenate([x_ref[:, s * SEG : (s + 1) * SEG] for s in range(NSEG)], axis=0)
    block = 384
    for c in range(N * SPAN // block):
        rows = iota((block, NSEG * TOK), 0) + c * block
        pick = jnp.where(
            rows == lanes[0], weights[0], jnp.where(rows == lanes[1], weights[1], 0.0)
        ).astype(BF16)
        out_ref[c * block : (c + 1) * block, :] = mm(pick, stacked).astype(BF16)


def send_tokens_kernel(ids_ref, x_ref, out_ref):
    send_rows(ids_ref, (1.0, 1.0), x_ref, out_ref)


def send_scaled_kernel(ids_ref, prob_ref, x_ref, out_ref):
    probs = [prob_ref[k : k + 1, :].astype(F32) for k in range(2)]
    weights = [jnp.concatenate([v] * NSEG, axis=1) for v in probs]
    send_rows(ids_ref, weights, x_ref, out_ref)


def unmix_rows(perm_ref, got_ref, rows_ref):
    perm = perm_ref[...]
    for g in range(NGROUP):
        part = mm(perm, got_ref[g * GROUP * SPAN : (g + 1) * GROUP * SPAN, :]).astype(BF16)
        for s in range(NSEG):
            rows_ref[s, g * GROWS : (g + 1) * GROWS, :] = part[s * GROWS : (s + 1) * GROWS]


def forward_kernel(
    dp_ref, perm_ref, got_ref, gate_w, up_w, gate_ref, up_ref, hidden_t, x0, x1, x2, x3, rows
):
    @pl.when(pl.program_id(0) == 0)
    def _():
        unmix_rows(perm_ref, got_ref, rows)
        for k, ref in enumerate((x0, x1, x2, x3)):
            which = lax.rem(dp_ref[0] + k, DP)
            ref[...] = rows[which].astype(F32).T.astype(BF16)

    gate = sum(mm(rows[s], gate_w[s * SEG : (s + 1) * SEG, :]) for s in range(NSEG))
    up = sum(mm(rows[s], up_w[s * SEG : (s + 1) * SEG, :]) for s in range(NSEG))
    gate_ref[...] = gate
    up_ref[...] = up
    hidden_t[...] = (gate * jax.nn.sigmoid(gate) * up).T.astype(BF16)


def backward_kernel(
    dp_ref, perm_ref, got_ref, down_w, gate_ref, up_ref, back_ref, q_ref, s0, s1, s2, s3, rows
):
    step = pl.program_id(0)

    @pl.when(step == 0)
    def _():
        unmix_rows(perm_ref, got_ref, rows)
        for k, ref in enumerate((s0, s1, s2, s3)):
            which = lax.rem(dp_ref[0] + k, DP)
            ref[...] = rows[which]
        q_ref[...] = jnp.zeros_like(q_ref)

    back_hidden = sum(mm_t(rows[s], down_w[:, s * SEG : (s + 1) * SEG]) for s in range(NSEG))
    gate = gate_ref[...]
    up = up_ref[...]
    sig = jax.nn.sigmoid(gate)
    activated = gate * sig
    hidden = (activated * up).astype(BF16).astype(F32)
    back_ref[0] = (back_hidden * up * sig * (1.0 + gate * (1.0 - sig))).astype(BF16)
    back_ref[1] = (back_hidden * activated).astype(BF16)
    q_ref[...] += jnp.broadcast_to(jnp.sum(hidden * back_hidden, axis=1, keepdims=True), q_ref.shape)


def return_kernel(mix_ref, mark_ref, back_ref, q_ref, gate_w, up_w, out_ref, rows):
    step = pl.program_id(0)
    part = (mm_t(back_ref[0], gate_w[...]) + mm_t(back_ref[1], up_w[...])).astype(BF16)
    for h in range(SEG // BSEG):
        rows[step * (SEG // BSEG) + h] = part[:, h * BSEG : (h + 1) * BSEG]

    @pl.when(step == pl.num_programs(0) - 1)
    def _():
        mix = mix_ref[...]
        for g in range(NGROUP):
            lo, hi = g * GROWS, (g + 1) * GROWS
            probs = (q_ref[lo:hi, 0:1] * mark_ref[...].astype(F32)).astype(BF16)
            stacked = jnp.concatenate([rows[s, lo:hi, :] for s in range(NBSEG)] + [probs], axis=0)
            out_ref[g * GROUP * BSPAN : (g + 1) * GROUP * BSPAN, :] = mm(mix, stacked).astype(BF16)


def combine_kernel(ids_ref, prob_ref, perm_ref, got_ref, tok_ref, gprob_ref, rows, probs):
    perm = perm_ref[...]
    for g in range(NGROUP):
        part = mm(perm, got_ref[g * GROUP * BSPAN : (g + 1) * GROUP * BSPAN, :])
        for s in range(NBSEG):
            rows[g * GROWS : (g + 1) * GROWS, s * BSEG : (s + 1) * BSEG] = part[
                s * GROWS : (s + 1) * GROWS
            ].astype(BF16)
        probs[g * GROUP : (g + 1) * GROUP, :] = part[NBSEG * GROWS : NBSEG * GROWS + GROUP]
    places = places_in_rows(ids_ref)
    at = [target * PER + slot for target, slot in places]
    columns = iota((TOK, ROWS), 1)
    pick = jnp.where((columns == at[0]) | (columns == at[1]), 1.0, 0.0).astype(BF16)
    tok_ref[...] = mm(pick, rows[...]).astype(BF16)
    home = probs[...].astype(BF16)
    result = []
    for k, (target, slot) in enumerate(places):
        owner = (iota((TOK, N), 1) == target).astype(F32).astype(BF16)
        line = mm(owner, home)
        value = jnp.sum(jnp.where(iota((TOK, BSEG), 1) == slot, line, 0.0), axis=1, keepdims=True)
        result.append(value / prob_ref[:, k : k + 1].astype(F32))
    gprob_ref[...] = jnp.where(iota((TOK, 2), 1) == 0, result[0], result[1]).astype(BF16)


def down_grad_kernel(dp_ref, hidden_t, s0, s1, s2, s3, out_ref, acc):
    step = pl.program_id(0)
    for k, ref in enumerate((s0, s1, s2, s3)):

        @pl.when(step == k)
        def _():
            term = mm(hidden_t[0], ref[...])
            acc[...] = term if k == 0 else acc[...] + term

    @pl.when(step == DP - 1)
    def _():
        out_ref[...] = acc[...].astype(BF16)


def gate_up_grad_kernel(dp_ref, back_ref, x0, x1, x2, x3, gate_out, up_out, acc):
    step = pl.program_id(0)
    for k, ref in enumerate((x0, x1, x2, x3)):

        @pl.when(step == k)
        def _():
            for m in range(2):
                term = mm(ref[...], back_ref[0, m])
                acc[m] = term if k == 0 else acc[m] + term

    @pl.when(step == DP - 1)
    def _():
        gate_out[...] = acc[0].astype(BF16)
        up_out[...] = acc[1].astype(BF16)


def shape(dims, kind=BF16):
    return jax.ShapeDtypeStruct(dims, kind)


def whole(dims):
    return pl.BlockSpec(dims, lambda *_: (0,) * len(dims))


def call(kernel, name, grid, in_specs, out_specs, out_shape, scratch=(), scalars=0, flops=0):
    return pl.pallas_call(
        kernel,
        name=name,
        grid_spec=pltpu.PrefetchScalarGridSpec(
            num_scalar_prefetch=scalars,
            grid=grid,
            in_specs=in_specs,
            out_specs=out_specs,
            scratch_shapes=list(scratch),
        ),
        out_shape=out_shape,
        compiler_params=pltpu.CompilerParams(vmem_limit_bytes=48 * 1024 * 1024),
        cost_estimate=pl.CostEstimate(flops=flops, bytes_accessed=8 << 20, transcendentals=0),
    )


def exchange(values):
    return lax.all_to_all(values, "expert", split_axis=0, concat_axis=0, tiled=True)


def spread(pieces):
    moved = [pieces[0]]
    for k in range(1, DP):
        moved.append(lax.ppermute(pieces[k], "dp", [(i, (i + k) % DP) for i in range(DP)]))
    return moved


def body(tokens, cotangent, gate_probs, expert_ids, gate_weight, up_weight, down_weight):
    gate_w, up_w, down_w = gate_weight[0], up_weight[0], down_weight[0]
    unmix = jnp.asarray(UNMIX, BF16)
    back_perm = jnp.asarray(BACK, BF16)
    mix = jnp.asarray(MIX, BF16)
    mark = jnp.asarray(MARK, BF16)
    dp = lax.axis_index("dp").astype(jnp.int32).reshape(1)
    ids_t = expert_ids.T
    probs_t = gate_probs.T

    send_x = call(
        send_tokens_kernel, "send_tokens", (1,), [whole((2, TOK)), whole((TOK, D))],
        whole((N * SPAN, SEG)), shape((N * SPAN, SEG)), flops=800 << 20,
    )(ids_t, tokens)
    got_x = exchange(send_x.reshape(N, SPAN, SEG)).reshape(N * SPAN, SEG)
    send_c = call(
        send_scaled_kernel, "send_scaled", (1,),
        [whole((2, TOK)), whole((2, TOK)), whole((TOK, D))],
        whole((N * SPAN, SEG)), shape((N * SPAN, SEG)), flops=800 << 20,
    )(ids_t, probs_t, cotangent)
    got_c = exchange(send_c.reshape(N, SPAN, SEG)).reshape(N * SPAN, SEG)

    gate, up, hidden_t, *x_pieces = call(
        forward_kernel, "forward", (NFB,),
        [
            whole(UNMIX.shape),
            whole((N * SPAN, SEG)),
            pl.BlockSpec((D, FB), lambda i, *_: (0, i)),
            pl.BlockSpec((D, FB), lambda i, *_: (0, i)),
        ],
        [
            pl.BlockSpec((ROWS, FB), lambda i, *_: (0, i)),
            pl.BlockSpec((ROWS, FB), lambda i, *_: (0, i)),
            pl.BlockSpec((FB, ROWS), lambda i, *_: (i, 0)),
        ]
        + [whole((SEG, ROWS))] * DP,
        [shape((ROWS, FF), F32), shape((ROWS, FF), F32), shape((FF, ROWS))]
        + [shape((SEG, ROWS))] * DP,
        scratch=[pltpu.VMEM((NSEG, ROWS, SEG), BF16)], scalars=1, flops=3000 << 20,
    )(dp, unmix, got_x, gate_w, up_w)
    x_pieces = spread(x_pieces)
    hidden_all = lax.all_gather(hidden_t, "dp", axis=0, tiled=True).reshape(DP, FF, ROWS)

    back, q, *s_pieces = call(
        backward_kernel, "backward", (NFB,),
        [
            whole(UNMIX.shape),
            whole((N * SPAN, SEG)),
            pl.BlockSpec((FB, D), lambda i, *_: (i, 0)),
            pl.BlockSpec((ROWS, FB), lambda i, *_: (0, i)),
            pl.BlockSpec((ROWS, FB), lambda i, *_: (0, i)),
        ],
        [pl.BlockSpec((2, ROWS, FB), lambda i, *_: (0, 0, i)), whole((ROWS, 128))]
        + [whole((ROWS, SEG))] * DP,
        [shape((2, ROWS, FF)), shape((ROWS, 128), F32)] + [shape((ROWS, SEG))] * DP,
        scratch=[pltpu.VMEM((NSEG, ROWS, SEG), BF16)], scalars=1, flops=2000 << 20,
    )(dp, unmix, got_c, down_w, gate, up)
    back_all = lax.all_gather(back.reshape(2 * ROWS, FF), "dp", axis=0, tiled=True)
    back_all = back_all.reshape(DP, 2, ROWS, FF)
    s_pieces = spread(s_pieces)

    send_b = call(
        return_kernel, "send_back", (NSEG,),
        [
            whole(MIX.shape),
            whole(MARK.shape),
            whole((2, ROWS, FF)),
            whole((ROWS, 128)),
            pl.BlockSpec((SEG, FF), lambda i, *_: (i, 0)),
            pl.BlockSpec((SEG, FF), lambda i, *_: (i, 0)),
        ],
        whole((N * BSPAN, BSEG)), shape((N * BSPAN, BSEG)),
        scratch=[pltpu.VMEM((NBSEG, ROWS, BSEG), BF16)], flops=3000 << 20,
    )(mix, mark, back, q, gate_w, up_w)
    got_b = exchange(send_b.reshape(N, BSPAN, BSEG)).reshape(N * BSPAN, BSEG)

    def other(i, dp_ref):
        return lax.rem(dp_ref[0] - i + DP, DP)

    grad_down = call(
        down_grad_kernel, "down_grad", (DP,),
        [pl.BlockSpec((1, FF, ROWS), lambda i, r: (other(i, r), 0, 0))] + [whole((ROWS, SEG))] * DP,
        whole((FF, SEG)), shape((FF, SEG)),
        scratch=[pltpu.VMEM((FF, SEG), F32)], scalars=1, flops=1200 << 20,
    )(dp, hidden_all, *s_pieces)
    grad_gate, grad_up = call(
        gate_up_grad_kernel, "gate_up_grad", (DP,),
        [pl.BlockSpec((1, 2, ROWS, FF), lambda i, r: (other(i, r), 0, 0, 0))]
        + [whole((SEG, ROWS))] * DP,
        [whole((SEG, FF))] * 2, [shape((SEG, FF))] * 2,
        scratch=[pltpu.VMEM((2, SEG, FF), F32)], scalars=1, flops=2400 << 20,
    )(dp, back_all, *x_pieces)
    grad_tokens, grad_probs = call(
        combine_kernel, "combine", (1,),
        [whole((TOK, 2)), whole((TOK, 2)), whole(BACK.shape), whole((N * BSPAN, BSEG))],
        [whole((TOK, D)), whole((TOK, 2))], [shape((TOK, D)), shape((TOK, 2))],
        scratch=[pltpu.VMEM((ROWS, D), BF16), pltpu.VMEM((N, BSEG), F32)], flops=1000 << 20,
    )(expert_ids, gate_probs, back_perm, got_b)
    return grad_tokens, grad_probs, grad_gate[None], grad_up[None], grad_down[None]


def solution(mesh):
    in_specs = (
        P(("dp", "expert"), None),
        P(("dp", "expert"), None),
        P(("dp", "expert"), None),
        P(("dp", "expert"), None),
        P("expert", None, None),
        P("expert", None, None),
        P("expert", None, None),
    )
    out_specs = (
        P(("dp", "expert"), None),
        P(("dp", "expert"), None),
        P("expert", "dp", None),
        P("expert", "dp", None),
        P("expert", None, "dp"),
    )
    return jax.shard_map(body, mesh=mesh, in_specs=in_specs, out_specs=out_specs, check_vma=False)
```

```python
import jax
import jax.numpy as jnp
import numpy as np
from jax import lax
from jax.experimental import pallas as pl
from jax.experimental.pallas import tpu as pltpu
from jax.sharding import PartitionSpec as P


F32 = jnp.float32
BF16 = jnp.bfloat16
N = 64
CAP = 3
PER = 2 * CAP
ROWS = N * PER
D = 2048
FF = 768
TOK = 128
DP = 4
SEG = 512
NSEG = D // SEG
SPAN = NSEG * PER
BSEG = 256
NBSEG = D // BSEG
BSPAN = NBSEG * PER + 8
GROUP = 8
GROWS = GROUP * PER
NGROUP = N // GROUP
FB = 256
NFB = FF // FB


def permutations():
    unmix = np.zeros((NSEG * GROWS, GROUP * SPAN), np.float32)
    back = np.zeros((NBSEG * GROWS + 16, GROUP * BSPAN), np.float32)
    mark = np.zeros((GROWS, BSEG), np.float32)
    spread = np.zeros((GROUP * BSPAN, GROWS), np.float32)
    for d in range(GROUP):
        for j in range(PER):
            row = d * PER + j
            mark[row, j] = 1
            spread[d * BSPAN + NBSEG * PER, row] = 1
            for s in range(NSEG):
                unmix[s * GROWS + row, d * SPAN + s * PER + j] = 1
            for s in range(NBSEG):
                back[s * GROWS + row, d * BSPAN + s * PER + j] = 1
        back[NBSEG * GROWS + d, d * BSPAN + NBSEG * PER] = 1
    mix = np.concatenate([back[: NBSEG * GROWS].T, spread], axis=1)
    return unmix, back, mix, mark


UNMIX, BACK, MIX, MARK = permutations()


def mm(a, b):
    return jnp.dot(a, b, preferred_element_type=F32)


def mm_t(a, b):
    return lax.dot_general(a, b, (((1,), (1,)), ((), ())), preferred_element_type=F32)


def iota(shape, dim):
    return lax.broadcasted_iota(jnp.int32, shape, dim)


def split_slot(ids):
    is_copy = (ids >= N).astype(jnp.int32)
    base = ids - N * is_copy
    target = jnp.where(ids >= N, jnp.bitwise_xor(base, N // 2), base)
    return target, is_copy * CAP


def places_in_lanes(ids_ref):
    ids = [ids_ref[k : k + 1, :] for k in range(2)]
    hot = [(iota((2 * N, TOK), 0) == v).astype(F32) for v in ids]
    before = (iota((TOK, TOK), 0) < iota((TOK, TOK), 1)).astype(F32).astype(BF16)
    count = mm((hot[0] + hot[1]).astype(BF16), before)
    out = []
    for k in range(2):
        rank = jnp.sum(count * hot[k], axis=0, keepdims=True).astype(jnp.int32)
        target, first = split_slot(ids[k])
        out.append((target, first + rank))
    return out


def places_in_rows(ids_ref):
    ids = [ids_ref[:, k : k + 1] for k in range(2)]
    hot = [(iota((TOK, 2 * N), 1) == v).astype(F32) for v in ids]
    before = (iota((TOK, TOK), 1) < iota((TOK, TOK), 0)).astype(F32).astype(BF16)
    count = mm(before, (hot[0] + hot[1]).astype(BF16))
    out = []
    for k in range(2):
        rank = jnp.sum(count * hot[k], axis=1, keepdims=True).astype(jnp.int32)
        target, first = split_slot(ids[k])
        out.append((target, first + rank))
    return out


def send_rows(ids_ref, weights, x_ref, out_ref):
    lanes = []
    for target, slot in places_in_lanes(ids_ref):
        at = target * SPAN + slot
        lanes.append(jnp.concatenate([at + s * PER for s in range(NSEG)], axis=1))
    stacked = jnp.concatenate([x_ref[:, s * SEG : (s + 1) * SEG] for s in range(NSEG)], axis=0)
    block = 384
    for c in range(N * SPAN // block):
        rows = iota((block, NSEG * TOK), 0) + c * block
        pick = jnp.where(
            rows == lanes[0], weights[0], jnp.where(rows == lanes[1], weights[1], 0.0)
        ).astype(BF16)
        out_ref[c * block : (c + 1) * block, :] = mm(pick, stacked).astype(BF16)


def send_tokens_kernel(ids_ref, x_ref, out_ref):
    send_rows(ids_ref, (1.0, 1.0), x_ref, out_ref)


def send_scaled_kernel(ids_ref, prob_ref, x_ref, out_ref):
    probs = [prob_ref[k : k + 1, :].astype(F32) for k in range(2)]
    weights = [jnp.concatenate([v] * NSEG, axis=1) for v in probs]
    send_rows(ids_ref, weights, x_ref, out_ref)


def unmix_rows(perm_ref, got_ref, rows_ref):
    perm = perm_ref[...]
    for g in range(NGROUP):
        part = mm(perm, got_ref[g * GROUP * SPAN : (g + 1) * GROUP * SPAN, :]).astype(BF16)
        for s in range(NSEG):
            rows_ref[s, g * GROWS : (g + 1) * GROWS, :] = part[s * GROWS : (s + 1) * GROWS]


def forward_kernel(
    dp_ref, perm_ref, got_ref, gate_w, up_w, gate_ref, up_ref, hidden_t, x0, x1, x2, x3, rows
):
    @pl.when(pl.program_id(0) == 0)
    def _():
        unmix_rows(perm_ref, got_ref, rows)
        for k, ref in enumerate((x0, x1, x2, x3)):
            which = lax.rem(dp_ref[0] + k, DP)
            ref[...] = rows[which].astype(F32).T.astype(BF16)

    gate = sum(mm(rows[s], gate_w[s * SEG : (s + 1) * SEG, :]) for s in range(NSEG))
    up = sum(mm(rows[s], up_w[s * SEG : (s + 1) * SEG, :]) for s in range(NSEG))
    gate_ref[...] = gate
    up_ref[...] = up
    hidden_t[...] = (gate * jax.nn.sigmoid(gate) * up).T.astype(BF16)


def backward_kernel(
    dp_ref, perm_ref, got_ref, down_w, gate_ref, up_ref, back_ref, q_ref, s0, s1, s2, s3, rows
):
    step = pl.program_id(0)

    @pl.when(step == 0)
    def _():
        unmix_rows(perm_ref, got_ref, rows)
        for k, ref in enumerate((s0, s1, s2, s3)):
            which = lax.rem(dp_ref[0] + k, DP)
            ref[...] = rows[which]
        q_ref[...] = jnp.zeros_like(q_ref)

    back_hidden = sum(mm_t(rows[s], down_w[:, s * SEG : (s + 1) * SEG]) for s in range(NSEG))
    gate = gate_ref[...]
    up = up_ref[...]
    sig = jax.nn.sigmoid(gate)
    activated = gate * sig
    hidden = (activated * up).astype(BF16).astype(F32)
    back_ref[0] = (back_hidden * up * sig * (1.0 + gate * (1.0 - sig))).astype(BF16)
    back_ref[1] = (back_hidden * activated).astype(BF16)
    q_ref[...] += jnp.broadcast_to(jnp.sum(hidden * back_hidden, axis=1, keepdims=True), q_ref.shape)


def return_kernel(mix_ref, mark_ref, back_ref, q_ref, gate_w, up_w, out_ref, rows):
    step = pl.program_id(0)
    part = (mm_t(back_ref[0], gate_w[...]) + mm_t(back_ref[1], up_w[...])).astype(BF16)
    for h in range(SEG // BSEG):
        rows[step * (SEG // BSEG) + h] = part[:, h * BSEG : (h + 1) * BSEG]

    @pl.when(step == pl.num_programs(0) - 1)
    def _():
        mix = mix_ref[...]
        for g in range(NGROUP):
            lo, hi = g * GROWS, (g + 1) * GROWS
            probs = (q_ref[lo:hi, 0:1] * mark_ref[...].astype(F32)).astype(BF16)
            stacked = jnp.concatenate([rows[s, lo:hi, :] for s in range(NBSEG)] + [probs], axis=0)
            out_ref[g * GROUP * BSPAN : (g + 1) * GROUP * BSPAN, :] = mm(mix, stacked).astype(BF16)


def combine_kernel(ids_ref, prob_ref, perm_ref, got_ref, tok_ref, gprob_ref, rows, probs):
    perm = perm_ref[...]
    for g in range(NGROUP):
        part = mm(perm, got_ref[g * GROUP * BSPAN : (g + 1) * GROUP * BSPAN, :])
        for s in range(NBSEG):
            rows[g * GROWS : (g + 1) * GROWS, s * BSEG : (s + 1) * BSEG] = part[
                s * GROWS : (s + 1) * GROWS
            ].astype(BF16)
        probs[g * GROUP : (g + 1) * GROUP, :] = part[NBSEG * GROWS : NBSEG * GROWS + GROUP]
    places = places_in_rows(ids_ref)
    at = [target * PER + slot for target, slot in places]
    columns = iota((TOK, ROWS), 1)
    pick = jnp.where((columns == at[0]) | (columns == at[1]), 1.0, 0.0).astype(BF16)
    tok_ref[...] = mm(pick, rows[...]).astype(BF16)
    home = probs[...].astype(BF16)
    result = []
    for k, (target, slot) in enumerate(places):
        owner = (iota((TOK, N), 1) == target).astype(F32).astype(BF16)
        line = mm(owner, home)
        value = jnp.sum(jnp.where(iota((TOK, BSEG), 1) == slot, line, 0.0), axis=1, keepdims=True)
        result.append(value / prob_ref[:, k : k + 1].astype(F32))
    gprob_ref[...] = jnp.where(iota((TOK, 2), 1) == 0, result[0], result[1]).astype(BF16)


def down_grad_kernel(dp_ref, hidden_t, s0, s1, s2, s3, out_ref, acc):
    step = pl.program_id(0)
    for k, ref in enumerate((s0, s1, s2, s3)):

        @pl.when(step == k)
        def _():
            term = mm(hidden_t[0], ref[...])
            acc[...] = term if k == 0 else acc[...] + term

    @pl.when(step == DP - 1)
    def _():
        out_ref[...] = acc[...].astype(BF16)


def gate_up_grad_kernel(dp_ref, back_ref, x0, x1, x2, x3, gate_out, up_out, acc):
    step = pl.program_id(0)
    for k, ref in enumerate((x0, x1, x2, x3)):

        @pl.when(step == k)
        def _():
            for m in range(2):
                term = mm(ref[...], back_ref[0, m])
                acc[m] = term if k == 0 else acc[m] + term

    @pl.when(step == DP - 1)
    def _():
        gate_out[...] = acc[0].astype(BF16)
        up_out[...] = acc[1].astype(BF16)


def shape(dims, kind=BF16):
    return pltpu.HBM(dims, kind)


def in_hbm(values):
    return pltpu.with_memory_space_constraint(values, pltpu.HBM)


def whole(dims):
    return pl.BlockSpec(dims, lambda *_: (0,) * len(dims))


def call(kernel, grid, in_specs, out_specs, out_shape, scratch=(), scalars=0, flops=0):
    return pl.pallas_call(
        kernel,
        grid_spec=pltpu.PrefetchScalarGridSpec(
            num_scalar_prefetch=scalars,
            grid=grid,
            in_specs=in_specs,
            out_specs=out_specs,
            scratch_shapes=list(scratch),
        ),
        out_shape=out_shape,
        compiler_params=pltpu.CompilerParams(vmem_limit_bytes=24 * 1024 * 1024),
        cost_estimate=pl.CostEstimate(flops=flops, bytes_accessed=8 << 20, transcendentals=0),
    )


def exchange(values):
    return lax.all_to_all(values, "expert", split_axis=0, concat_axis=0, tiled=True)


def gather(values):
    return lax.all_gather(values, "dp", axis=0, tiled=True)


def spread(pieces):
    moved = [pieces[0]]
    for k in range(1, DP):
        moved.append(lax.ppermute(pieces[k], "dp", [(i, (i + k) % DP) for i in range(DP)]))
    return moved


def body(tokens, cotangent, gate_probs, expert_ids, gate_weight, up_weight, down_weight):
    gate_w, up_w, down_w = in_hbm(gate_weight[0]), in_hbm(up_weight[0]), in_hbm(down_weight[0])
    unmix = jnp.asarray(UNMIX, BF16)
    back_perm = jnp.asarray(BACK, BF16)
    mix = jnp.asarray(MIX, BF16)
    mark = jnp.asarray(MARK, BF16)
    dp = lax.axis_index("dp").astype(jnp.int32).reshape(1)
    ids_t = expert_ids.T
    probs_t = gate_probs.T

    send_x = call(
        send_tokens_kernel, (1,), [whole((2, TOK)), whole((TOK, D))],
        whole((N * SPAN, SEG)), shape((N * SPAN, SEG)), flops=800 << 20,
    )(ids_t, tokens)
    got_x = exchange(send_x.reshape(N, SPAN, SEG)).reshape(N * SPAN, SEG)
    send_c = call(
        send_scaled_kernel, (1,),
        [whole((2, TOK)), whole((2, TOK)), whole((TOK, D))],
        whole((N * SPAN, SEG)), shape((N * SPAN, SEG)), flops=800 << 20,
    )(ids_t, probs_t, cotangent)
    got_c = exchange(send_c.reshape(N, SPAN, SEG)).reshape(N * SPAN, SEG)

    gate, up, hidden_t, *x_pieces = call(
        forward_kernel, (NFB,),
        [
            whole(UNMIX.shape),
            whole((N * SPAN, SEG)),
            pl.BlockSpec((D, FB), lambda i, *_: (0, i)),
            pl.BlockSpec((D, FB), lambda i, *_: (0, i)),
        ],
        [
            pl.BlockSpec((ROWS, FB), lambda i, *_: (0, i)),
            pl.BlockSpec((ROWS, FB), lambda i, *_: (0, i)),
            pl.BlockSpec((FB, ROWS), lambda i, *_: (i, 0)),
        ]
        + [whole((SEG, ROWS))] * DP,
        [shape((ROWS, FF), F32), shape((ROWS, FF), F32), shape((FF, ROWS))]
        + [shape((SEG, ROWS))] * DP,
        scratch=[pltpu.VMEM((NSEG, ROWS, SEG), BF16)], scalars=1, flops=3000 << 20,
    )(dp, unmix, got_x, gate_w, up_w)
    x_pieces = spread(x_pieces)
    hidden_all = gather(hidden_t).reshape(DP, FF, ROWS)

    back, q, *s_pieces = call(
        backward_kernel, (NFB,),
        [
            whole(UNMIX.shape),
            whole((N * SPAN, SEG)),
            pl.BlockSpec((FB, D), lambda i, *_: (i, 0)),
            pl.BlockSpec((ROWS, FB), lambda i, *_: (0, i)),
            pl.BlockSpec((ROWS, FB), lambda i, *_: (0, i)),
        ],
        [pl.BlockSpec((2, ROWS, FB), lambda i, *_: (0, 0, i)), whole((ROWS, 128))]
        + [whole((ROWS, SEG))] * DP,
        [shape((2, ROWS, FF)), shape((ROWS, 128), F32)] + [shape((ROWS, SEG))] * DP,
        scratch=[pltpu.VMEM((NSEG, ROWS, SEG), BF16)], scalars=1, flops=2000 << 20,
    )(dp, unmix, got_c, down_w, in_hbm(gate), in_hbm(up))
    back_all = gather(back.reshape(2 * ROWS, FF))
    back_all = back_all.reshape(DP, 2, ROWS, FF)
    s_pieces = spread(s_pieces)

    send_b = call(
        return_kernel, (NSEG,),
        [
            whole(MIX.shape),
            whole(MARK.shape),
            whole((2, ROWS, FF)),
            whole((ROWS, 128)),
            pl.BlockSpec((SEG, FF), lambda i, *_: (i, 0)),
            pl.BlockSpec((SEG, FF), lambda i, *_: (i, 0)),
        ],
        whole((N * BSPAN, BSEG)), shape((N * BSPAN, BSEG)),
        scratch=[pltpu.VMEM((NBSEG, ROWS, BSEG), BF16)], flops=3000 << 20,
    )(mix, mark, in_hbm(back), in_hbm(q), gate_w, up_w)
    got_b = exchange(send_b.reshape(N, BSPAN, BSEG)).reshape(N * BSPAN, BSEG)

    def other(i, dp_ref):
        return lax.rem(dp_ref[0] - i + DP, DP)

    grad_down = call(
        down_grad_kernel, (DP,),
        [pl.BlockSpec((1, FF, ROWS), lambda i, r: (other(i, r), 0, 0))] + [whole((ROWS, SEG))] * DP,
        whole((FF, SEG)), shape((FF, SEG)),
        scratch=[pltpu.VMEM((FF, SEG), F32)], scalars=1, flops=1200 << 20,
    )(dp, in_hbm(hidden_all), *s_pieces)
    grad_gate, grad_up = call(
        gate_up_grad_kernel, (DP,),
        [pl.BlockSpec((1, 2, ROWS, FF), lambda i, r: (other(i, r), 0, 0, 0))]
        + [whole((SEG, ROWS))] * DP,
        [whole((SEG, FF))] * 2, [shape((SEG, FF))] * 2,
        scratch=[pltpu.VMEM((2, SEG, FF), F32)], scalars=1, flops=2400 << 20,
    )(dp, in_hbm(back_all), *x_pieces)
    grad_tokens, grad_probs = call(
        combine_kernel, (1,),
        [whole((TOK, 2)), whole((TOK, 2)), whole(BACK.shape), whole((N * BSPAN, BSEG))],
        [whole((TOK, D)), whole((TOK, 2))], [shape((TOK, D)), shape((TOK, 2))],
        scratch=[pltpu.VMEM((ROWS, D), BF16), pltpu.VMEM((N, BSEG), F32)], flops=1000 << 20,
    )(expert_ids, gate_probs, back_perm, got_b)
    return grad_tokens, grad_probs, grad_gate[None], grad_up[None], grad_down[None]


def solution(mesh):
    in_specs = (
        P(("dp", "expert"), None),
        P(("dp", "expert"), None),
        P(("dp", "expert"), None),
        P(("dp", "expert"), None),
        P("expert", None, None),
        P("expert", None, None),
        P("expert", None, None),
    )
    out_specs = (
        P(("dp", "expert"), None),
        P(("dp", "expert"), None),
        P("expert", "dp", None),
        P("expert", "dp", None),
        P("expert", None, "dp"),
    )

    return jax.shard_map(body, mesh=mesh, in_specs=in_specs, out_specs=out_specs, check_vma=False)
```

```python
import jax
import jax.numpy as jnp
import numpy as np
from jax import lax
from jax.experimental import pallas as pl
from jax.experimental.pallas import tpu as pltpu
from jax.sharding import PartitionSpec as P


F32 = jnp.float32
BF16 = jnp.bfloat16
N = 64
CAP = 3
PER = 2 * CAP
ROWS = N * PER
D = 2048
FF = 768
TOK = 128
DP = 4
SEG = 512
NSEG = D // SEG
SPAN = NSEG * PER
BSEG = 256
NBSEG = D // BSEG
BSPAN = NBSEG * PER + 8
GROUP = 8
GROWS = GROUP * PER
NGROUP = N // GROUP
FB = 256
NFB = FF // FB


def permutations():
    unmix = np.zeros((NSEG * GROWS, GROUP * SPAN), np.float32)
    back = np.zeros((NBSEG * GROWS + 16, GROUP * BSPAN), np.float32)
    mark = np.zeros((GROWS, BSEG), np.float32)
    spread = np.zeros((GROUP * BSPAN, GROWS), np.float32)
    for d in range(GROUP):
        for j in range(PER):
            row = d * PER + j
            mark[row, j] = 1
            spread[d * BSPAN + NBSEG * PER, row] = 1
            for s in range(NSEG):
                unmix[s * GROWS + row, d * SPAN + s * PER + j] = 1
            for s in range(NBSEG):
                back[s * GROWS + row, d * BSPAN + s * PER + j] = 1
        back[NBSEG * GROWS + d, d * BSPAN + NBSEG * PER] = 1
    mix = np.concatenate([back[: NBSEG * GROWS].T, spread], axis=1)
    return unmix, back, mix, mark


UNMIX, BACK, MIX, MARK = permutations()


def mm(a, b):
    return jnp.dot(a, b, preferred_element_type=F32)


def mm_t(a, b):
    return lax.dot_general(a, b, (((1,), (1,)), ((), ())), preferred_element_type=F32)


def iota(shape, dim):
    return lax.broadcasted_iota(jnp.int32, shape, dim)


def split_slot(ids):
    is_copy = (ids >= N).astype(jnp.int32)
    base = ids - N * is_copy
    target = jnp.where(ids >= N, jnp.bitwise_xor(base, N // 2), base)
    return target, is_copy * CAP


def places_in_lanes(ids_ref):
    ids = [ids_ref[k : k + 1, :] for k in range(2)]
    hot = [(iota((2 * N, TOK), 0) == v).astype(F32) for v in ids]
    before = (iota((TOK, TOK), 0) < iota((TOK, TOK), 1)).astype(F32).astype(BF16)
    count = mm((hot[0] + hot[1]).astype(BF16), before)
    out = []
    for k in range(2):
        rank = jnp.sum(count * hot[k], axis=0, keepdims=True).astype(jnp.int32)
        target, first = split_slot(ids[k])
        out.append((target, first + rank))
    return out


def places_in_rows(ids_ref):
    ids = [ids_ref[:, k : k + 1] for k in range(2)]
    hot = [(iota((TOK, 2 * N), 1) == v).astype(F32) for v in ids]
    before = (iota((TOK, TOK), 1) < iota((TOK, TOK), 0)).astype(F32).astype(BF16)
    count = mm(before, (hot[0] + hot[1]).astype(BF16))
    out = []
    for k in range(2):
        rank = jnp.sum(count * hot[k], axis=1, keepdims=True).astype(jnp.int32)
        target, first = split_slot(ids[k])
        out.append((target, first + rank))
    return out


def send_rows(ids_ref, weights, x_ref, out_ref):
    lanes = []
    for target, slot in places_in_lanes(ids_ref):
        at = target * SPAN + slot
        lanes.append(jnp.concatenate([at + s * PER for s in range(NSEG)], axis=1))
    stacked = jnp.concatenate([x_ref[:, s * SEG : (s + 1) * SEG] for s in range(NSEG)], axis=0)
    block = 384
    for c in range(N * SPAN // block):
        rows = iota((block, NSEG * TOK), 0) + c * block
        pick = jnp.where(
            rows == lanes[0], weights[0], jnp.where(rows == lanes[1], weights[1], 0.0)
        ).astype(BF16)
        out_ref[c * block : (c + 1) * block, :] = mm(pick, stacked).astype(BF16)


def send_tokens_kernel(ids_ref, x_ref, out_ref):
    send_rows(ids_ref, (1.0, 1.0), x_ref, out_ref)


def send_scaled_kernel(ids_ref, prob_ref, x_ref, out_ref):
    probs = [prob_ref[k : k + 1, :].astype(F32) for k in range(2)]
    weights = [jnp.concatenate([v] * NSEG, axis=1) for v in probs]
    send_rows(ids_ref, weights, x_ref, out_ref)


def unmix_rows(perm_ref, got_ref, rows_ref):
    perm = perm_ref[...]
    for g in range(NGROUP):
        part = mm(perm, got_ref[g * GROUP * SPAN : (g + 1) * GROUP * SPAN, :]).astype(BF16)
        for s in range(NSEG):
            rows_ref[s, g * GROWS : (g + 1) * GROWS, :] = part[s * GROWS : (s + 1) * GROWS]


def unmix_kernel(dp_ref, perm_ref, got_ref, rows, x0, x1, x2, x3):
    unmix_rows(perm_ref, got_ref, rows)
    for k, ref in enumerate((x0, x1, x2, x3)):
        which = lax.rem(dp_ref[0] + k, DP)
        ref[...] = rows[which].astype(F32).T.astype(BF16)


def forward_kernel(rows, gate_w, up_w, gate_ref, up_ref, hidden_t):
    gate = sum(mm(rows[s], gate_w[s * SEG : (s + 1) * SEG, :]) for s in range(NSEG))
    up = sum(mm(rows[s], up_w[s * SEG : (s + 1) * SEG, :]) for s in range(NSEG))
    gate_ref[...] = gate
    up_ref[...] = up
    hidden_t[...] = (gate * jax.nn.sigmoid(gate) * up).T.astype(BF16)


def backward_kernel(
    dp_ref, perm_ref, got_ref, down_w, gate_ref, up_ref, back_ref, q_ref, s0, s1, s2, s3, rows
):
    step = pl.program_id(0)

    @pl.when(step == 0)
    def _():
        unmix_rows(perm_ref, got_ref, rows)
        for k, ref in enumerate((s0, s1, s2, s3)):
            which = lax.rem(dp_ref[0] + k, DP)
            ref[...] = rows[which]
        q_ref[...] = jnp.zeros_like(q_ref)

    back_hidden = sum(mm_t(rows[s], down_w[:, s * SEG : (s + 1) * SEG]) for s in range(NSEG))
    gate = gate_ref[...]
    up = up_ref[...]
    sig = jax.nn.sigmoid(gate)
    activated = gate * sig
    hidden = (activated * up).astype(BF16).astype(F32)
    back_ref[0] = (back_hidden * up * sig * (1.0 + gate * (1.0 - sig))).astype(BF16)
    back_ref[1] = (back_hidden * activated).astype(BF16)
    q_ref[...] += jnp.broadcast_to(jnp.sum(hidden * back_hidden, axis=1, keepdims=True), q_ref.shape)


def return_kernel(mix_ref, mark_ref, back_ref, q_ref, gate_w, up_w, out_ref, rows):
    step = pl.program_id(0)
    part = (mm_t(back_ref[0], gate_w[...]) + mm_t(back_ref[1], up_w[...])).astype(BF16)
    for h in range(SEG // BSEG):
        rows[step * (SEG // BSEG) + h] = part[:, h * BSEG : (h + 1) * BSEG]

    @pl.when(step == pl.num_programs(0) - 1)
    def _():
        mix = mix_ref[...]
        for g in range(NGROUP):
            lo, hi = g * GROWS, (g + 1) * GROWS
            probs = (q_ref[lo:hi, 0:1] * mark_ref[...].astype(F32)).astype(BF16)
            stacked = jnp.concatenate([rows[s, lo:hi, :] for s in range(NBSEG)] + [probs], axis=0)
            out_ref[g * GROUP * BSPAN : (g + 1) * GROUP * BSPAN, :] = mm(mix, stacked).astype(BF16)


def combine_kernel(
    ids_ref, ids_t_ref, prob_ref, perm_ref, got_ref, tok_ref, gprob_ref, rows, probs
):
    perm = perm_ref[...]
    for g in range(NGROUP):
        part = mm(perm, got_ref[g * GROUP * BSPAN : (g + 1) * GROUP * BSPAN, :])
        for s in range(NBSEG):
            rows[g * GROWS : (g + 1) * GROWS, s * BSEG : (s + 1) * BSEG] = part[
                s * GROWS : (s + 1) * GROWS
            ].astype(BF16)
        probs[g * GROUP : (g + 1) * GROUP, :] = part[NBSEG * GROWS : NBSEG * GROWS + GROUP]
    at = [target * PER + slot for target, slot in places_in_rows(ids_ref)]
    columns = iota((TOK, ROWS), 1)
    pick = jnp.where((columns == at[0]) | (columns == at[1]), 1.0, 0.0).astype(BF16)
    tok_ref[...] = mm(pick, rows[...]).astype(BF16)
    home = probs[...][:, :TOK].T.astype(BF16)
    for k, (target, slot) in enumerate(places_in_lanes(ids_t_ref)):
        owner = (iota((N, TOK), 0) == target).astype(F32).astype(BF16)
        line = mm(home, owner)
        value = jnp.sum(jnp.where(iota((TOK, TOK), 0) == slot, line, 0.0), axis=0, keepdims=True)
        gprob_ref[k : k + 1, :] = (value / prob_ref[k : k + 1, :].astype(F32)).astype(BF16)


def down_grad_kernel(h0, h1, h3, h2_low, h2_high, s0, s1, s2, s3, out_ref):
    acc = mm(h0[...], s0[...]) + mm(h1[...], s1[...]) + mm(h3[...], s3[...])
    half = FF // 2
    out_ref[:half] = (acc[:half] + mm(h2_low[...], s2[...])).astype(BF16)
    out_ref[half:] = (acc[half:] + mm(h2_high[...], s2[...])).astype(BF16)


def grad_first_kernel(b0, b1, b3, x0, x1, x3, acc):
    acc[0] = mm(x0[...], b0[0]) + mm(x1[...], b1[0]) + mm(x3[...], b3[0])


def grad_last_kernel(acc, gate_b, up_b, x2, gate_out, up_out):
    gate_out[...] = (acc[0] + mm(x2[...], gate_b[0])).astype(BF16)
    up_out[...] = (acc[1] + mm(x2[...], up_b[0])).astype(BF16)


def shape(dims, kind=BF16):
    return pltpu.HBM(dims, kind)


def in_hbm(values):
    return pltpu.with_memory_space_constraint(values, pltpu.HBM)


def whole(dims):
    return pl.BlockSpec(dims, lambda *_: (0,) * len(dims))


def call(kernel, grid, in_specs, out_specs, out_shape, scratch=(), scalars=0, flops=0):
    return pl.pallas_call(
        kernel,
        grid_spec=pltpu.PrefetchScalarGridSpec(
            num_scalar_prefetch=scalars,
            grid=grid,
            in_specs=in_specs,
            out_specs=out_specs,
            scratch_shapes=list(scratch),
        ),
        out_shape=out_shape,
        compiler_params=pltpu.CompilerParams(vmem_limit_bytes=24 * 1024 * 1024),
        cost_estimate=pl.CostEstimate(flops=flops, bytes_accessed=8 << 20, transcendentals=0),
    )


def exchange(values):
    return lax.all_to_all(values, "expert", split_axis=0, concat_axis=0, tiled=True)


def shift(values, k):
    return lax.ppermute(values, "dp", [(i, (i + k) % DP) for i in range(DP)])


def spread(pieces):
    return [pieces[0]] + [shift(pieces[k], k) for k in range(1, DP)]


def around(values):
    after = shift(values, 1)
    before = shift(values, DP - 1)
    half = values.shape[0] // 2
    low = shift(after[:half], 1)
    high = shift(before[half:], DP - 1)
    return after, before, low, high


def body(tokens, cotangent, gate_probs, expert_ids, gate_weight, up_weight, down_weight):
    gate_w, up_w, down_w = in_hbm(gate_weight[0]), in_hbm(up_weight[0]), in_hbm(down_weight[0])
    unmix = jnp.asarray(UNMIX, BF16)
    back_perm = jnp.asarray(BACK, BF16)
    mix = jnp.asarray(MIX, BF16)
    mark = jnp.asarray(MARK, BF16)
    dp = lax.axis_index("dp").astype(jnp.int32).reshape(1)
    ids_t = expert_ids.T
    probs_t = gate_probs.T

    send_x = call(
        send_tokens_kernel, (1,), [whole((2, TOK)), whole((TOK, D))],
        whole((N * SPAN, SEG)), shape((N * SPAN, SEG)), flops=800 << 20,
    )(in_hbm(ids_t), in_hbm(tokens))
    got_x = exchange(send_x.reshape(N, SPAN, SEG)).reshape(N * SPAN, SEG)
    send_c = call(
        send_scaled_kernel, (1,),
        [whole((2, TOK)), whole((2, TOK)), whole((TOK, D))],
        whole((N * SPAN, SEG)), shape((N * SPAN, SEG)), flops=800 << 20,
    )(ids_t, probs_t, cotangent)
    got_c = exchange(send_c.reshape(N, SPAN, SEG)).reshape(N * SPAN, SEG)

    rows, *x_pieces = call(
        unmix_kernel, (1,),
        [whole(UNMIX.shape), whole((N * SPAN, SEG))],
        [whole((NSEG, ROWS, SEG))] + [whole((SEG, ROWS))] * DP,
        [shape((NSEG, ROWS, SEG))] + [shape((SEG, ROWS))] * DP,
        scalars=1, flops=300 << 20,
    )(dp, unmix, got_x)
    x_pieces = spread(x_pieces)
    gate, up, hidden_t = call(
        forward_kernel, (NFB,),
        [
            whole((NSEG, ROWS, SEG)),
            pl.BlockSpec((D, FB), lambda i, *_: (0, i)),
            pl.BlockSpec((D, FB), lambda i, *_: (0, i)),
        ],
        [
            pl.BlockSpec((ROWS, FB), lambda i, *_: (0, i)),
            pl.BlockSpec((ROWS, FB), lambda i, *_: (0, i)),
            pl.BlockSpec((FB, ROWS), lambda i, *_: (i, 0)),
        ],
        [shape((ROWS, FF), F32), shape((ROWS, FF), F32), shape((FF, ROWS))],
        flops=3000 << 20,
    )(in_hbm(rows), gate_w, up_w)
    h1, h3, h_low, h_high = around(hidden_t)

    back, q, *s_pieces = call(
        backward_kernel, (NFB,),
        [
            whole(UNMIX.shape),
            whole((N * SPAN, SEG)),
            pl.BlockSpec((FB, D), lambda i, *_: (i, 0)),
            pl.BlockSpec((ROWS, FB), lambda i, *_: (0, i)),
            pl.BlockSpec((ROWS, FB), lambda i, *_: (0, i)),
        ],
        [pl.BlockSpec((2, ROWS, FB), lambda i, *_: (0, 0, i)), whole((ROWS, 128))]
        + [whole((ROWS, SEG))] * DP,
        [shape((2, ROWS, FF)), shape((ROWS, 128), F32)] + [shape((ROWS, SEG))] * DP,
        scratch=[pltpu.VMEM((NSEG, ROWS, SEG), BF16)], scalars=1, flops=2000 << 20,
    )(dp, unmix, got_c, down_w, in_hbm(gate), in_hbm(up))
    b1, b3, b_low, b_high = around(back)
    s_pieces = spread(s_pieces)

    send_b = call(
        return_kernel, (NSEG,),
        [
            whole(MIX.shape),
            whole(MARK.shape),
            whole((2, ROWS, FF)),
            whole((ROWS, 128)),
            pl.BlockSpec((SEG, FF), lambda i, *_: (i, 0)),
            pl.BlockSpec((SEG, FF), lambda i, *_: (i, 0)),
        ],
        whole((N * BSPAN, BSEG)), shape((N * BSPAN, BSEG)),
        scratch=[pltpu.VMEM((NBSEG, ROWS, BSEG), BF16)], flops=3000 << 20,
    )(mix, mark, in_hbm(back), in_hbm(q), gate_w, up_w)
    got_b = exchange(send_b.reshape(N, BSPAN, BSEG)).reshape(N * BSPAN, BSEG)

    grad_down = call(
        down_grad_kernel, (1,),
        [whole((FF, ROWS))] * 3 + [whole((FF // 2, ROWS))] * 2 + [whole((ROWS, SEG))] * DP,
        whole((FF, SEG)), shape((FF, SEG)), flops=1200 << 20,
    )(hidden_t, h1, h3, h_low, h_high, *s_pieces)
    acc = call(
        grad_first_kernel, (2,),
        [pl.BlockSpec((1, ROWS, FF), lambda i: (i, 0, 0))] * 3 + [whole((SEG, ROWS))] * 3,
        pl.BlockSpec((1, SEG, FF), lambda i: (i, 0, 0)), shape((2, SEG, FF), F32),
        flops=1800 << 20,
    )(back, b1, b3, x_pieces[0], x_pieces[1], x_pieces[3])
    grad_gate, grad_up = call(
        grad_last_kernel, (NFB,),
        [
            pl.BlockSpec((2, SEG, FB), lambda i: (0, 0, i)),
            pl.BlockSpec((1, ROWS, FB), lambda i: (0, 0, i)),
            pl.BlockSpec((1, ROWS, FB), lambda i: (0, 0, i)),
            whole((SEG, ROWS)),
        ],
        [pl.BlockSpec((SEG, FB), lambda i: (0, i))] * 2, [shape((SEG, FF))] * 2,
        flops=600 << 20,
    )(in_hbm(acc), b_low, b_high, x_pieces[2])
    grad_tokens, grad_probs = call(
        combine_kernel, (1,),
        [
            whole((TOK, 2)),
            whole((2, TOK)),
            whole((2, TOK)),
            whole(BACK.shape),
            whole((N * BSPAN, BSEG)),
        ],
        [whole((TOK, D)), whole((2, TOK))], [shape((TOK, D)), shape((2, TOK))],
        scratch=[pltpu.VMEM((ROWS, D), BF16), pltpu.VMEM((N, BSEG), F32)], flops=1000 << 20,
    )(expert_ids, ids_t, probs_t, in_hbm(back_perm), got_b)
    return grad_tokens, grad_probs.T, grad_gate[None], grad_up[None], grad_down[None]


def solution(mesh):
    in_specs = (
        P(("dp", "expert"), None),
        P(("dp", "expert"), None),
        P(("dp", "expert"), None),
        P(("dp", "expert"), None),
        P("expert", None, None),
        P("expert", None, None),
        P("expert", None, None),
    )
    out_specs = (
        P(("dp", "expert"), None),
        P(("dp", "expert"), None),
        P("expert", "dp", None),
        P("expert", "dp", None),
        P("expert", None, "dp"),
    )

    return jax.shard_map(body, mesh=mesh, in_specs=in_specs, out_specs=out_specs, check_vma=False)
```

```python
import jax
import jax.numpy as jnp
import numpy as np
from jax import lax
from jax.experimental import pallas as pl
from jax.experimental.pallas import tpu as pltpu
from jax.sharding import PartitionSpec as P


F32 = jnp.float32
BF16 = jnp.bfloat16
N = 64
CAP = 3
PER = 2 * CAP
ROWS = N * PER
D = 2048
FF = 768
TOK = 128
DP = 4
SEG = 512
NSEG = D // SEG
SPAN = NSEG * PER
TILE = 128
NU = D // (4 * TILE)
BROWS = 8
BCOLS = (3 * NU + 1) * TILE
GROUP = 8
GROWS = GROUP * PER
NGROUP = N // GROUP
FB = 256
NFB = FF // FB


def permutations():
    unmix = np.zeros((NSEG * GROWS, GROUP * SPAN), np.float32)
    pack = np.zeros((3 * GROUP * BROWS, 4 * GROWS), np.float32)
    probs = np.zeros((GROUP * BROWS, GROWS), np.float32)
    for d in range(GROUP):
        for j in range(PER):
            row = d * PER + j
            probs[d * BROWS + j, row] = 1
            for s in range(NSEG):
                unmix[s * GROWS + row, d * SPAN + s * PER + j] = 1
            for v in range(4):
                c, r = divmod(v * PER + j, BROWS)
                pack[(c * GROUP + d) * BROWS + r, v * GROWS + row] = 1
    return unmix, pack, np.ascontiguousarray(pack.T), probs


UNMIX, PACK, UNPACK, PROBS = permutations()


def mm(a, b):
    return jnp.dot(a, b, preferred_element_type=F32)


def mm_t(a, b):
    return lax.dot_general(a, b, (((1,), (1,)), ((), ())), preferred_element_type=F32)


def iota(shape, dim):
    return lax.broadcasted_iota(jnp.int32, shape, dim)


def split_slot(ids):
    is_copy = (ids >= N).astype(jnp.int32)
    base = ids - N * is_copy
    target = jnp.where(ids >= N, jnp.bitwise_xor(base, N // 2), base)
    return target, is_copy * CAP


def places_in_lanes(ids_ref):
    ids = [ids_ref[k : k + 1, :] for k in range(2)]
    hot = [(iota((2 * N, TOK), 0) == v).astype(F32) for v in ids]
    before = (iota((TOK, TOK), 0) < iota((TOK, TOK), 1)).astype(F32).astype(BF16)
    count = mm((hot[0] + hot[1]).astype(BF16), before)
    out = []
    for k in range(2):
        rank = jnp.sum(count * hot[k], axis=0, keepdims=True).astype(jnp.int32)
        target, first = split_slot(ids[k])
        out.append((target, first + rank))
    return out


def places_in_rows(ids_ref):
    ids = [ids_ref[:, k : k + 1] for k in range(2)]
    hot = [(iota((TOK, 2 * N), 1) == v).astype(F32) for v in ids]
    before = (iota((TOK, TOK), 1) < iota((TOK, TOK), 0)).astype(F32).astype(BF16)
    count = mm(before, (hot[0] + hot[1]).astype(BF16))
    out = []
    for k in range(2):
        rank = jnp.sum(count * hot[k], axis=1, keepdims=True).astype(jnp.int32)
        target, first = split_slot(ids[k])
        out.append((target, first + rank))
    return out


def send_rows(ids_ref, weights, x_ref, out_ref):
    lanes = []
    for target, slot in places_in_lanes(ids_ref):
        at = target * SPAN + slot
        lanes.append(jnp.concatenate([at + s * PER for s in range(NSEG)], axis=1))
    stacked = jnp.concatenate([x_ref[:, s * SEG : (s + 1) * SEG] for s in range(NSEG)], axis=0)
    block = 384
    for c in range(N * SPAN // block):
        rows = iota((block, NSEG * TOK), 0) + c * block
        pick = jnp.where(
            rows == lanes[0], weights[0], jnp.where(rows == lanes[1], weights[1], 0.0)
        ).astype(BF16)
        out_ref[c * block : (c + 1) * block, :] = mm(pick, stacked).astype(BF16)


def send_tokens_kernel(ids_ref, x_ref, out_ref):
    send_rows(ids_ref, (1.0, 1.0), x_ref, out_ref)


def send_scaled_kernel(ids_ref, prob_ref, x_ref, out_ref):
    probs = [prob_ref[k : k + 1, :].astype(F32) for k in range(2)]
    weights = [jnp.concatenate([v] * NSEG, axis=1) for v in probs]
    send_rows(ids_ref, weights, x_ref, out_ref)


def unmix_rows(perm_ref, got_ref, rows_ref):
    perm = perm_ref[...]
    for g in range(NGROUP):
        part = mm(perm, got_ref[g * GROUP * SPAN : (g + 1) * GROUP * SPAN, :]).astype(BF16)
        for s in range(NSEG):
            rows_ref[s, g * GROWS : (g + 1) * GROWS, :] = part[s * GROWS : (s + 1) * GROWS]


def unmix_kernel(dp_ref, perm_ref, got_ref, rows, x0, x1, x2, x3):
    unmix_rows(perm_ref, got_ref, rows)
    for k, ref in enumerate((x0, x1, x2, x3)):
        which = lax.rem(dp_ref[0] + k, DP)
        ref[...] = rows[which].astype(F32).T.astype(BF16)


def forward_kernel(
    rows, gate_hbm, up_hbm, gate_ref, up_ref, hidden_low, hidden_high, gate_w, up_w, sems
):
    half = FF // 2
    copies = []
    for i in range(2):
        at = pl.ds(i * half, half)
        for m, (source, target) in enumerate(((gate_hbm, gate_w), (up_hbm, up_w))):
            copies.append(
                pltpu.make_async_copy(source.at[:, at], target.at[:, at], sems.at[2 * i + m])
            )
            copies[-1].start()
    for i, out in enumerate((hidden_low, hidden_high)):
        at = slice(i * half, (i + 1) * half)
        copies[2 * i].wait()
        gate = sum(mm(rows[s], gate_w[s * SEG : (s + 1) * SEG, at]) for s in range(NSEG))
        copies[2 * i + 1].wait()
        up = sum(mm(rows[s], up_w[s * SEG : (s + 1) * SEG, at]) for s in range(NSEG))
        gate_ref[:, at] = gate
        up_ref[:, at] = up
        out[...] = (gate * jax.nn.sigmoid(gate) * up).T.astype(BF16)


def backward_kernel(
    dp_ref, perm_ref, got_ref, down_hbm, gate_hbm, up_hbm,
    back_ref, q_ref, gate_out, up_out, s0, s1, s2, s3, rows, down_w, gate_ref, up_ref, sems, loads,
):
    arriving = []
    for i in range(NFB):
        at = pl.ds(i * FB, FB)
        pairs = (
            (down_hbm.at[at], down_w.at[at]),
            (gate_hbm.at[:, at], gate_ref.at[:, at]),
            (up_hbm.at[:, at], up_ref.at[:, at]),
        )
        for m, (source, target) in enumerate(pairs):
            arriving.append(pltpu.make_async_copy(source, target, loads.at[3 * i + m]))
            arriving[-1].start()
    unmix_rows(perm_ref, got_ref, rows)
    copies = []
    for k, ref in enumerate((s0, s1, s2, s3)):
        which = lax.rem(dp_ref[0] + k, DP)
        copies.append(pltpu.make_async_copy(rows.at[which], ref, sems.at[k]))
    total = jnp.zeros((ROWS, 1), F32)
    for i in range(NFB):
        at = slice(i * FB, (i + 1) * FB)
        for copy in arriving[3 * i : 3 * i + 3]:
            copy.wait()
        back_hidden = sum(mm_t(rows[s], down_w[at, s * SEG : (s + 1) * SEG]) for s in range(NSEG))
        gate = gate_ref[:, at]
        up = up_ref[:, at]
        sig = jax.nn.sigmoid(gate)
        activated = gate * sig
        hidden = (activated * up).astype(BF16).astype(F32)
        back_ref[0, :, at] = (back_hidden * up * sig * (1.0 + gate * (1.0 - sig))).astype(BF16)
        back_ref[1, :, at] = (back_hidden * activated).astype(BF16)
        total += jnp.sum(hidden * back_hidden, axis=1, keepdims=True)
        if i == 0:
            for copy in copies:
                copy.start()
    for m, ref in enumerate((gate_out, up_out)):
        copies.append(pltpu.make_async_copy(back_ref.at[m], ref, sems.at[DP + m]))
        copies[-1].start()
    q_ref[...] = jnp.broadcast_to(total, q_ref.shape)
    for copy in copies:
        copy.wait()


def send_back_kernel(pack_ref, probs_ref, back_ref, q_ref, gate_w, up_w, out_ref, rows, sent, sems):
    for i in range(NSEG):
        at = slice(i * SEG, (i + 1) * SEG)
        rows[:, at] = (mm_t(back_ref[0], gate_w[at, :]) + mm_t(back_ref[1], up_w[at, :])).astype(BF16)
    pack = pack_ref[...]
    height = GROUP * BROWS
    copies = []
    for g in range(NGROUP):
        lo, hi = g * GROWS, (g + 1) * GROWS
        stacked = jnp.concatenate(
            [
                jnp.concatenate(
                    [rows[lo:hi, (4 * u + v) * TILE : (4 * u + v + 1) * TILE] for u in range(NU)],
                    axis=1,
                )
                for v in range(4)
            ],
            axis=0,
        )
        part = mm(pack, stacked).astype(BF16)
        top = g * height
        for u in range(NU):
            for c in range(3):
                col = (3 * u + c) * TILE
                sent[top : top + height, col : col + TILE] = part[
                    c * height : (c + 1) * height, u * TILE : (u + 1) * TILE
                ]
        sent[top : top + height, 3 * NU * TILE :] = mm(
            probs_ref[...], q_ref[lo:hi, :].astype(BF16)
        ).astype(BF16)
        half = slice(top, top + height)
        copies.append(pltpu.make_async_copy(sent.at[half], out_ref.at[half], sems.at[g]))
        copies[-1].start()
    for copy in copies:
        copy.wait()


def combine_kernel(ids_ref, ids_t_ref, prob_ref, perm_ref, got_ref, tok_ref, gprob_ref, rows):
    perm = perm_ref[...]
    height = GROUP * BROWS
    for g in range(NGROUP):
        top = g * height
        stacked = jnp.concatenate(
            [
                jnp.concatenate(
                    [
                        got_ref[top : top + height, (3 * u + c) * TILE : (3 * u + c + 1) * TILE]
                        for u in range(NU)
                    ],
                    axis=1,
                )
                for c in range(3)
            ],
            axis=0,
        )
        part = mm(perm, stacked).astype(BF16)
        for u in range(NU):
            for v in range(4):
                col = (4 * u + v) * TILE
                rows[g * GROWS : (g + 1) * GROWS, col : col + TILE] = part[
                    v * GROWS : (v + 1) * GROWS, u * TILE : (u + 1) * TILE
                ]
    at = [target * PER + slot for target, slot in places_in_rows(ids_ref)]
    columns = iota((TOK, ROWS), 1)
    pick = jnp.where((columns == at[0]) | (columns == at[1]), 1.0, 0.0).astype(BF16)
    tok_ref[...] = mm(pick, rows[...]).astype(BF16)
    home = got_ref[:, 3 * NU * TILE :].astype(F32)
    line = iota((N * BROWS, TOK), 0)
    for k, (target, slot) in enumerate(places_in_lanes(ids_t_ref)):
        hit = jnp.where(line == target * BROWS + slot, home, 0.0)
        value = jnp.sum(hit, axis=0, keepdims=True)
        gprob_ref[k : k + 1, :] = (value / prob_ref[k : k + 1, :].astype(F32)).astype(BF16)


def down_grad_kernel(*refs):
    out_ref = refs[-1]
    pieces = refs[2 * DP : 3 * DP]
    half = FF // 2
    for m in range(2):
        acc = sum(mm(refs[m * DP + k][...], pieces[k][...]) for k in range(DP))
        out_ref[m * half : (m + 1) * half] = acc.astype(BF16)


def grad_first_kernel(g0, g1, g3, u0, u1, u3, x0, x1, x3, acc):
    acc[0] = mm(x0[...], g0[...]) + mm(x1[...], g1[...]) + mm(x3[...], g3[...])
    acc[1] = mm(x0[...], u0[...]) + mm(x1[...], u1[...]) + mm(x3[...], u3[...])


def grad_last_kernel(acc, gate_b, up_b, x2, gate_out, up_out):
    gate_out[...] = (acc[0] + mm(x2[...], gate_b[...])).astype(BF16)
    up_out[...] = (acc[1] + mm(x2[...], up_b[...])).astype(BF16)


def shape(dims, kind=BF16):
    return pltpu.HBM(dims, kind)


def near(dims, kind=BF16):
    return pltpu.VMEM(dims, kind)


def in_hbm(values):
    return pltpu.with_memory_space_constraint(values, pltpu.HBM)


def in_vmem(values):
    return pltpu.with_memory_space_constraint(values, pltpu.VMEM)


def call(kernel, out_shape, scratch=(), scalars=0, far=(), by_hand=(), flops=0):
    def run(*args):
        space = [pl.ANY if i in far else pltpu.VMEM for i in range(len(args))]
        space[:scalars] = [pltpu.SMEM] * scalars
        outs = [pl.ANY if i in by_hand else pltpu.VMEM for i in range(len(out_shape))]
        return pl.pallas_call(
            kernel,
            in_specs=[pl.BlockSpec(memory_space=v) for v in space],
            out_specs=[pl.BlockSpec(memory_space=v) for v in outs],
            out_shape=list(out_shape),
            scratch_shapes=list(scratch),
            compiler_params=pltpu.CompilerParams(vmem_limit_bytes=24 * 1024 * 1024),
            cost_estimate=pl.CostEstimate(flops=flops, bytes_accessed=8 << 20, transcendentals=0),
        )(*args)

    return run


def exchange(values):
    return lax.all_to_all(values, "expert", split_axis=0, concat_axis=0, tiled=True)


def shift(values, k):
    return lax.ppermute(values, "dp", [(i, (i + k) % DP) for i in range(DP)])


def spread(pieces):
    return [pieces[0]] + [shift(pieces[k], k) for k in range(1, DP)]


def around(low, high):
    low1 = shift(low, 1)
    high3 = shift(high, DP - 1)
    low3 = shift(low, DP - 1)
    high1 = shift(high, 1)
    low2 = shift(low1, 1)
    high2 = shift(high3, DP - 1)
    return (low, low1, low2, low3), (high, high1, high2, high3)


def body(tokens, cotangent, gate_probs, expert_ids, gate_weight, up_weight, down_weight):
    dp = lax.axis_index("dp").astype(jnp.int32).reshape(1)
    ids_t = expert_ids.T
    probs_t = gate_probs.T

    (send_x,) = call(send_tokens_kernel, [shape((N * SPAN, SEG))], flops=800 << 20)(
        in_hbm(ids_t), in_hbm(tokens)
    )
    got_x = exchange(send_x.reshape(N, SPAN, SEG)).reshape(N * SPAN, SEG)
    (send_c,) = call(send_scaled_kernel, [shape((N * SPAN, SEG))], flops=800 << 20)(
        ids_t, probs_t, cotangent
    )
    got_c = exchange(send_c.reshape(N, SPAN, SEG)).reshape(N * SPAN, SEG)

    unmix, pack, unpack, probs_perm = [jnp.asarray(v, BF16) for v in (UNMIX, PACK, UNPACK, PROBS)]

    rows, *x_pieces = call(
        unmix_kernel,
        [near((NSEG, ROWS, SEG))] + [shape((SEG, ROWS))] * DP,
        scalars=1, flops=300 << 20,
    )(dp, unmix, got_x)
    x_pieces = spread(x_pieces)
    gate, up, hidden_low, hidden_high = call(
        forward_kernel,
        [shape((ROWS, FF), F32)] * 2 + [shape((FF // 2, ROWS))] * 2,
        scratch=[
            pltpu.VMEM((D, FF), BF16),
            pltpu.VMEM((D, FF), BF16),
            pltpu.SemaphoreType.DMA((4,)),
        ],
        far=(1, 2), flops=3000 << 20,
    )(in_vmem(rows), in_hbm(gate_weight[0]), in_hbm(up_weight[0]))
    h_low, h_high = around(hidden_low, hidden_high)

    back_near, q, back_gate, back_up, *s_pieces = call(
        backward_kernel,
        [near((2, ROWS, FF)), near((ROWS, TILE), F32)]
        + [shape((ROWS, FF))] * 2
        + [shape((ROWS, SEG))] * DP,
        scratch=[
            pltpu.VMEM((NSEG, ROWS, SEG), BF16),
            pltpu.VMEM((FF, D), BF16),
            pltpu.VMEM((ROWS, FF), F32),
            pltpu.VMEM((ROWS, FF), F32),
            pltpu.SemaphoreType.DMA((DP + 2,)),
            pltpu.SemaphoreType.DMA((3 * NFB,)),
        ],
        scalars=1, far=(3, 4, 5), by_hand=(2, 3, 4, 5, 6, 7), flops=2000 << 20,
    )(dp, unmix, got_c, in_hbm(down_weight[0]), in_hbm(gate), in_hbm(up))
    b_gate, b_up = around(back_gate, back_up)
    s_pieces = spread(s_pieces)

    (send_b,) = call(
        send_back_kernel, [shape((N * BROWS, BCOLS))],
        scratch=[
            pltpu.VMEM((ROWS, D), BF16),
            pltpu.VMEM((N * BROWS, BCOLS), BF16),
            pltpu.SemaphoreType.DMA((NGROUP,)),
        ],
        by_hand=(0,), flops=3000 << 20,
    )(pack, probs_perm, in_vmem(back_near), in_vmem(q), in_vmem(gate_weight[0]), in_vmem(up_weight[0]))
    got_b = exchange(send_b.reshape(N, BROWS, BCOLS)).reshape(N * BROWS, BCOLS)

    (acc,) = call(grad_first_kernel, [near((2, SEG, FF), F32)], flops=1800 << 20)(
        *(b[k] for b in (b_gate, b_up) for k in (0, 1, 3)), x_pieces[0], x_pieces[1], x_pieces[3]
    )
    (grad_down,) = call(down_grad_kernel, [shape((FF, SEG))], flops=1200 << 20)(
        *h_low, *h_high, *s_pieces
    )
    grad_gate, grad_up = call(grad_last_kernel, [shape((SEG, FF))] * 2, flops=600 << 20)(
        in_vmem(acc), b_gate[2], b_up[2], x_pieces[2]
    )
    grad_tokens, grad_probs = call(
        combine_kernel, [shape((TOK, D)), shape((2, TOK))],
        scratch=[pltpu.VMEM((ROWS, D), BF16)], flops=1000 << 20,
    )(expert_ids, ids_t, probs_t, unpack, got_b)
    return grad_tokens, grad_probs.T, grad_gate[None], grad_up[None], grad_down[None]


def solution(mesh):
    in_specs = (
        P(("dp", "expert"), None),
        P(("dp", "expert"), None),
        P(("dp", "expert"), None),
        P(("dp", "expert"), None),
        P("expert", None, None),
        P("expert", None, None),
        P("expert", None, None),
    )
    out_specs = (
        P(("dp", "expert"), None),
        P(("dp", "expert"), None),
        P("expert", "dp", None),
        P("expert", "dp", None),
        P("expert", None, "dp"),
    )

    return jax.shard_map(body, mesh=mesh, in_specs=in_specs, out_specs=out_specs, check_vma=False)
```

```python
import jax
import jax.numpy as jnp
import numpy as np
from jax import lax
from jax.experimental import pallas as pl
from jax.experimental.pallas import tpu as pltpu
from jax.sharding import PartitionSpec as P


F32 = jnp.float32
BF16 = jnp.bfloat16
N = 64
CAP = 3
PER = 2 * CAP
ROWS = N * PER
D = 2048
FF = 768
TOK = 128
DP = 4
SEG = 512
NSEG = D // SEG
SPAN = NSEG * PER
TILE = 128
NU = D // (4 * TILE)
BROWS = 8
BCOLS = (3 * NU + 1) * TILE
GROUP = 8
GROWS = GROUP * PER
NGROUP = N // GROUP
FB = 256
NFB = FF // FB


def permutations():
    unmix = np.zeros((NSEG * GROWS, GROUP * SPAN), np.float32)
    pack = np.zeros((3 * GROUP * BROWS, 4 * GROWS), np.float32)
    probs = np.zeros((GROUP * BROWS, GROWS), np.float32)
    for d in range(GROUP):
        for j in range(PER):
            row = d * PER + j
            probs[d * BROWS + j, row] = 1
            for s in range(NSEG):
                unmix[s * GROWS + row, d * SPAN + s * PER + j] = 1
            for v in range(4):
                c, r = divmod(v * PER + j, BROWS)
                pack[(c * GROUP + d) * BROWS + r, v * GROWS + row] = 1
    return unmix, pack, np.ascontiguousarray(pack.T), probs


UNMIX, PACK, UNPACK, PROBS = permutations()


def mm(a, b):
    return jnp.dot(a, b, preferred_element_type=F32)


def mm_t(a, b):
    return lax.dot_general(a, b, (((1,), (1,)), ((), ())), preferred_element_type=F32)


def iota(shape, dim):
    return lax.broadcasted_iota(jnp.int32, shape, dim)


def split_slot(ids):
    is_copy = (ids >= N).astype(jnp.int32)
    base = ids - N * is_copy
    target = jnp.where(ids >= N, jnp.bitwise_xor(base, N // 2), base)
    return target, is_copy * CAP


def places_in_lanes(ids_ref):
    ids = [ids_ref[k : k + 1, :] for k in range(2)]
    hot = [(iota((2 * N, TOK), 0) == v).astype(F32) for v in ids]
    before = (iota((TOK, TOK), 0) < iota((TOK, TOK), 1)).astype(F32).astype(BF16)
    count = mm((hot[0] + hot[1]).astype(BF16), before)
    out = []
    for k in range(2):
        rank = jnp.sum(count * hot[k], axis=0, keepdims=True).astype(jnp.int32)
        target, first = split_slot(ids[k])
        out.append((target, first + rank))
    return out


def places_in_rows(ids_ref):
    ids = [ids_ref[:, k : k + 1] for k in range(2)]
    hot = [(iota((TOK, 2 * N), 1) == v).astype(F32) for v in ids]
    before = (iota((TOK, TOK), 1) < iota((TOK, TOK), 0)).astype(F32).astype(BF16)
    count = mm(before, (hot[0] + hot[1]).astype(BF16))
    out = []
    for k in range(2):
        rank = jnp.sum(count * hot[k], axis=1, keepdims=True).astype(jnp.int32)
        target, first = split_slot(ids[k])
        out.append((target, first + rank))
    return out


def send_rows(ids_ref, weights, x_ref, out_ref):
    lanes = []
    for target, slot in places_in_lanes(ids_ref):
        at = target * SPAN + slot
        lanes.append(jnp.concatenate([at + s * PER for s in range(NSEG)], axis=1))
    stacked = jnp.concatenate([x_ref[:, s * SEG : (s + 1) * SEG] for s in range(NSEG)], axis=0)
    block = 384
    for c in range(N * SPAN // block):
        rows = iota((block, NSEG * TOK), 0) + c * block
        pick = jnp.where(
            rows == lanes[0], weights[0], jnp.where(rows == lanes[1], weights[1], 0.0)
        ).astype(BF16)
        out_ref[c * block : (c + 1) * block, :] = mm(pick, stacked).astype(BF16)


def send_tokens_kernel(ids_ref, x_ref, out_ref):
    send_rows(ids_ref, (1.0, 1.0), x_ref, out_ref)


def send_scaled_kernel(ids_ref, prob_ref, x_ref, out_ref):
    probs = [prob_ref[k : k + 1, :].astype(F32) for k in range(2)]
    weights = [jnp.concatenate([v] * NSEG, axis=1) for v in probs]
    send_rows(ids_ref, weights, x_ref, out_ref)


def unmix_rows(perm_ref, got_ref, rows_ref):
    perm = perm_ref[...]
    for g in range(NGROUP):
        part = mm(perm, got_ref[g * GROUP * SPAN : (g + 1) * GROUP * SPAN, :]).astype(BF16)
        for s in range(NSEG):
            rows_ref[s, g * GROWS : (g + 1) * GROWS, :] = part[s * GROWS : (s + 1) * GROWS]


def unmix_kernel(dp_ref, perm_ref, got_ref, rows, x0, x1, x2, x3):
    unmix_rows(perm_ref, got_ref, rows)
    for k, ref in enumerate((x0, x1, x2, x3)):
        which = lax.rem(dp_ref[0] + k, DP)
        ref[...] = rows[which].astype(F32).T.astype(BF16)


def forward_kernel(
    rows, gate_hbm, up_hbm, gate_ref, up_ref, hidden_low, hidden_high, gate_w, up_w, sems
):
    half = FF // 2
    copies = []
    for i in range(2):
        at = pl.ds(i * half, half)
        for m, (source, target) in enumerate(((gate_hbm, gate_w), (up_hbm, up_w))):
            copies.append(
                pltpu.make_async_copy(source.at[:, at], target.at[:, at], sems.at[2 * i + m])
            )
            copies[-1].start()
    for i, out in enumerate((hidden_low, hidden_high)):
        at = slice(i * half, (i + 1) * half)
        copies[2 * i].wait()
        gate = sum(mm(rows[s], gate_w[s * SEG : (s + 1) * SEG, at]) for s in range(NSEG))
        copies[2 * i + 1].wait()
        up = sum(mm(rows[s], up_w[s * SEG : (s + 1) * SEG, at]) for s in range(NSEG))
        gate_ref[:, at] = gate.astype(BF16)
        up_ref[:, at] = up.astype(BF16)
        out[...] = (gate * jax.nn.sigmoid(gate) * up).T.astype(BF16)


def backward_kernel(
    dp_ref, perm_ref, got_ref, down_hbm, gate_hbm, up_hbm,
    back_ref, q_ref, gate_out, up_out, s0, s1, s2, s3, rows, down_w, gate_ref, up_ref, sems, loads,
):
    arriving = []
    for i in range(NFB):
        at = pl.ds(i * FB, FB)
        pairs = (
            (down_hbm.at[at], down_w.at[at]),
            (gate_hbm.at[:, at], gate_ref.at[:, at]),
            (up_hbm.at[:, at], up_ref.at[:, at]),
        )
        for m, (source, target) in enumerate(pairs):
            arriving.append(pltpu.make_async_copy(source, target, loads.at[3 * i + m]))
            arriving[-1].start()
    unmix_rows(perm_ref, got_ref, rows)
    copies = []
    for k, ref in enumerate((s0, s1, s2, s3)):
        which = lax.rem(dp_ref[0] + k, DP)
        copies.append(pltpu.make_async_copy(rows.at[which], ref, sems.at[k]))
    total = jnp.zeros((ROWS, 1), F32)
    for i in range(NFB):
        at = slice(i * FB, (i + 1) * FB)
        for copy in arriving[3 * i : 3 * i + 3]:
            copy.wait()
        back_hidden = sum(mm_t(rows[s], down_w[at, s * SEG : (s + 1) * SEG]) for s in range(NSEG))
        gate = gate_ref[:, at].astype(F32)
        up = up_ref[:, at].astype(F32)
        sig = jax.nn.sigmoid(gate)
        activated = gate * sig
        hidden = (activated * up).astype(BF16).astype(F32)
        back_ref[0, :, at] = (back_hidden * up * sig * (1.0 + gate * (1.0 - sig))).astype(BF16)
        back_ref[1, :, at] = (back_hidden * activated).astype(BF16)
        total += jnp.sum(hidden * back_hidden, axis=1, keepdims=True)
        if i == 0:
            for copy in copies:
                copy.start()
        for m, ref in enumerate((gate_out, up_out)):
            part = pl.ds(i * FB, FB)
            copies.append(
                pltpu.make_async_copy(
                    back_ref.at[m, :, part], ref.at[:, part], sems.at[DP + 2 * i + m]
                )
            )
            copies[-1].start()
    q_ref[...] = jnp.broadcast_to(total, q_ref.shape)
    for copy in copies:
        copy.wait()


def send_back_kernel(pack_ref, probs_ref, back_ref, q_ref, gate_w, up_w, out_ref, rows, sent, sems):
    for i in range(NSEG):
        at = slice(i * SEG, (i + 1) * SEG)
        rows[:, at] = (mm_t(back_ref[0], gate_w[at, :]) + mm_t(back_ref[1], up_w[at, :])).astype(BF16)
    pack = pack_ref[...]
    height = GROUP * BROWS
    copies = []
    for g in range(NGROUP):
        lo, hi = g * GROWS, (g + 1) * GROWS
        stacked = jnp.concatenate(
            [
                jnp.concatenate(
                    [rows[lo:hi, (4 * u + v) * TILE : (4 * u + v + 1) * TILE] for u in range(NU)],
                    axis=1,
                )
                for v in range(4)
            ],
            axis=0,
        )
        part = mm(pack, stacked).astype(BF16)
        top = g * height
        for u in range(NU):
            for c in range(3):
                col = (3 * u + c) * TILE
                sent[top : top + height, col : col + TILE] = part[
                    c * height : (c + 1) * height, u * TILE : (u + 1) * TILE
                ]
        sent[top : top + height, 3 * NU * TILE :] = mm(
            probs_ref[...], q_ref[lo:hi, :].astype(BF16)
        ).astype(BF16)
        half = slice(top, top + height)
        copies.append(pltpu.make_async_copy(sent.at[half], out_ref.at[half], sems.at[g]))
        copies[-1].start()
    for copy in copies:
        copy.wait()


def combine_kernel(ids_ref, ids_t_ref, prob_ref, perm_ref, got_ref, tok_ref, gprob_ref, rows):
    perm = perm_ref[...]
    height = GROUP * BROWS
    for g in range(NGROUP):
        top = g * height
        stacked = jnp.concatenate(
            [
                jnp.concatenate(
                    [
                        got_ref[top : top + height, (3 * u + c) * TILE : (3 * u + c + 1) * TILE]
                        for u in range(NU)
                    ],
                    axis=1,
                )
                for c in range(3)
            ],
            axis=0,
        )
        part = mm(perm, stacked).astype(BF16)
        for u in range(NU):
            for v in range(4):
                col = (4 * u + v) * TILE
                rows[g * GROWS : (g + 1) * GROWS, col : col + TILE] = part[
                    v * GROWS : (v + 1) * GROWS, u * TILE : (u + 1) * TILE
                ]
    at = [target * PER + slot for target, slot in places_in_rows(ids_ref)]
    columns = iota((TOK, ROWS), 1)
    pick = jnp.where((columns == at[0]) | (columns == at[1]), 1.0, 0.0).astype(BF16)
    tok_ref[...] = mm(pick, rows[...]).astype(BF16)
    home = got_ref[:, 3 * NU * TILE :].astype(F32)
    line = iota((N * BROWS, TOK), 0)
    for k, (target, slot) in enumerate(places_in_lanes(ids_t_ref)):
        hit = jnp.where(line == target * BROWS + slot, home, 0.0)
        value = jnp.sum(hit, axis=0, keepdims=True)
        gprob_ref[k : k + 1, :] = (value / prob_ref[k : k + 1, :].astype(F32)).astype(BF16)


def down_grad_kernel(*refs):
    out_ref = refs[-1]
    pieces = refs[2 * DP : 3 * DP]
    half = FF // 2
    for m in range(2):
        acc = sum(mm(refs[m * DP + k][...], pieces[k][...]) for k in range(DP))
        out_ref[m * half : (m + 1) * half] = acc.astype(BF16)


def grad_first_kernel(g0, g1, g3, u0, u1, u3, x0, x1, x3, acc):
    acc[0] = mm(x0[...], g0[...]) + mm(x1[...], g1[...]) + mm(x3[...], g3[...])
    acc[1] = mm(x0[...], u0[...]) + mm(x1[...], u1[...]) + mm(x3[...], u3[...])


def grad_last_kernel(acc, gate_b, up_b, x2, gate_out, up_out):
    gate_out[...] = (acc[0] + mm(x2[...], gate_b[...])).astype(BF16)
    up_out[...] = (acc[1] + mm(x2[...], up_b[...])).astype(BF16)


def shape(dims, kind=BF16):
    return pltpu.HBM(dims, kind)


def near(dims, kind=BF16):
    return pltpu.VMEM(dims, kind)


def in_hbm(values):
    return pltpu.with_memory_space_constraint(values, pltpu.HBM)


def in_vmem(values):
    return pltpu.with_memory_space_constraint(values, pltpu.VMEM)


def call(kernel, out_shape, scratch=(), scalars=0, far=(), by_hand=(), flops=0):
    def run(*args):
        space = [pl.ANY if i in far else pltpu.VMEM for i in range(len(args))]
        space[:scalars] = [pltpu.SMEM] * scalars
        outs = [pl.ANY if i in by_hand else pltpu.VMEM for i in range(len(out_shape))]
        return pl.pallas_call(
            kernel,
            in_specs=[pl.BlockSpec(memory_space=v) for v in space],
            out_specs=[pl.BlockSpec(memory_space=v) for v in outs],
            out_shape=list(out_shape),
            scratch_shapes=list(scratch),
            compiler_params=pltpu.CompilerParams(vmem_limit_bytes=24 * 1024 * 1024),
            cost_estimate=pl.CostEstimate(flops=flops, bytes_accessed=8 << 20, transcendentals=0),
        )(*args)

    return run


def exchange(values):
    return lax.all_to_all(values, "expert", split_axis=0, concat_axis=0, tiled=True)


def shift(values, k):
    return lax.ppermute(values, "dp", [(i, (i + k) % DP) for i in range(DP)])


def spread(pieces):
    return [pieces[0]] + [shift(pieces[k], k) for k in range(1, DP)]


def around(low, high):
    low1 = shift(low, 1)
    high3 = shift(high, DP - 1)
    low3 = shift(low, DP - 1)
    high1 = shift(high, 1)
    low2 = shift(low1, 1)
    high2 = shift(high3, DP - 1)
    return (low, low1, low2, low3), (high, high1, high2, high3)


def body(tokens, cotangent, gate_probs, expert_ids, gate_weight, up_weight, down_weight):
    dp = lax.axis_index("dp").astype(jnp.int32).reshape(1)
    ids_t = expert_ids.T
    probs_t = gate_probs.T

    (send_x,) = call(send_tokens_kernel, [shape((N * SPAN, SEG))], flops=800 << 20)(
        in_hbm(ids_t), in_hbm(tokens)
    )
    got_x = exchange(send_x.reshape(N, SPAN, SEG)).reshape(N * SPAN, SEG)
    (send_c,) = call(send_scaled_kernel, [shape((N * SPAN, SEG))], flops=800 << 20)(
        ids_t, probs_t, cotangent
    )
    got_c = exchange(send_c.reshape(N, SPAN, SEG)).reshape(N * SPAN, SEG)

    unmix, pack, unpack, probs_perm = [jnp.asarray(v, BF16) for v in (UNMIX, PACK, UNPACK, PROBS)]

    rows, *x_pieces = call(
        unmix_kernel,
        [near((NSEG, ROWS, SEG))] + [shape((SEG, ROWS))] * DP,
        scalars=1, flops=300 << 20,
    )(dp, unmix, got_x)
    x_pieces = spread(x_pieces)
    gate, up, hidden_low, hidden_high = call(
        forward_kernel,
        [shape((ROWS, FF))] * 2 + [shape((FF // 2, ROWS))] * 2,
        scratch=[
            pltpu.VMEM((D, FF), BF16),
            pltpu.VMEM((D, FF), BF16),
            pltpu.SemaphoreType.DMA((4,)),
        ],
        far=(1, 2), flops=3000 << 20,
    )(in_vmem(rows), in_hbm(gate_weight[0]), in_hbm(up_weight[0]))
    h_low, h_high = around(hidden_low, hidden_high)

    back_near, q, back_gate, back_up, *s_pieces = call(
        backward_kernel,
        [near((2, ROWS, FF)), near((ROWS, TILE), F32)]
        + [shape((ROWS, FF))] * 2
        + [shape((ROWS, SEG))] * DP,
        scratch=[
            pltpu.VMEM((NSEG, ROWS, SEG), BF16),
            pltpu.VMEM((FF, D), BF16),
            pltpu.VMEM((ROWS, FF), BF16),
            pltpu.VMEM((ROWS, FF), BF16),
            pltpu.SemaphoreType.DMA((DP + 2 * NFB,)),
            pltpu.SemaphoreType.DMA((3 * NFB,)),
        ],
        scalars=1, far=(3, 4, 5), by_hand=(2, 3, 4, 5, 6, 7), flops=2000 << 20,
    )(dp, unmix, got_c, in_hbm(down_weight[0]), in_hbm(gate), in_hbm(up))
    b_gate, b_up = around(back_gate, back_up)
    s_pieces = spread(s_pieces)

    (send_b,) = call(
        send_back_kernel, [shape((N * BROWS, BCOLS))],
        scratch=[
            pltpu.VMEM((ROWS, D), BF16),
            pltpu.VMEM((N * BROWS, BCOLS), BF16),
            pltpu.SemaphoreType.DMA((NGROUP,)),
        ],
        by_hand=(0,), flops=3000 << 20,
    )(pack, probs_perm, in_vmem(back_near), in_vmem(q), in_vmem(gate_weight[0]), in_vmem(up_weight[0]))
    got_b = exchange(send_b.reshape(N, BROWS, BCOLS)).reshape(N * BROWS, BCOLS)

    (acc,) = call(grad_first_kernel, [near((2, SEG, FF), F32)], flops=1800 << 20)(
        *(b[k] for b in (b_gate, b_up, x_pieces) for k in (0, 1, 3))
    )
    (grad_down,) = call(down_grad_kernel, [shape((FF, SEG))], flops=1200 << 20)(
        *h_low, *h_high, *s_pieces
    )
    grad_gate, grad_up = call(grad_last_kernel, [shape((SEG, FF))] * 2, flops=600 << 20)(
        in_vmem(acc), b_gate[2], b_up[2], x_pieces[2]
    )
    grad_tokens, grad_probs = call(
        combine_kernel, [shape((TOK, D)), shape((2, TOK))],
        scratch=[pltpu.VMEM((ROWS, D), BF16)], flops=1000 << 20,
    )(expert_ids, ids_t, probs_t, unpack, got_b)
    return grad_tokens, grad_probs.T, grad_gate[None], grad_up[None], grad_down[None]


def solution(mesh):
    in_specs = (
        P(("dp", "expert"), None),
        P(("dp", "expert"), None),
        P(("dp", "expert"), None),
        P(("dp", "expert"), None),
        P("expert", None, None),
        P("expert", None, None),
        P("expert", None, None),
    )
    out_specs = (
        P(("dp", "expert"), None),
        P(("dp", "expert"), None),
        P("expert", "dp", None),
        P("expert", "dp", None),
        P("expert", None, "dp"),
    )

    return jax.shard_map(body, mesh=mesh, in_specs=in_specs, out_specs=out_specs, check_vma=False)
```

```python
import jax
import jax.numpy as jnp
import numpy as np
from jax import lax
from jax.experimental import pallas as pl
from jax.experimental.pallas import tpu as pltpu
from jax.sharding import PartitionSpec as P


F32 = jnp.float32
BF16 = jnp.bfloat16
N = 64
CAP = 3
PER = 2 * CAP
ROWS = N * PER
D = 2048
FF = 768
TOK = 128
DP = 4
SEG = 512
NSEG = D // SEG
SPAN = NSEG * PER
TILE = 128
NU = D // (4 * TILE)
BROWS = 8
BCOLS = (3 * NU + 1) * TILE
GROUP = 8
GROWS = GROUP * PER
NGROUP = N // GROUP
FB = 256
NFB = FF // FB


def permutations():
    unmix = np.zeros((NSEG * GROWS, GROUP * SPAN), np.float32)
    pack = np.zeros((3 * GROUP * BROWS, 4 * GROWS), np.float32)
    probs = np.zeros((GROUP * BROWS, GROWS), np.float32)
    for d in range(GROUP):
        for j in range(PER):
            row = d * PER + j
            probs[d * BROWS + j, row] = 1
            for s in range(NSEG):
                unmix[s * GROWS + row, d * SPAN + s * PER + j] = 1
            for v in range(4):
                c, r = divmod(v * PER + j, BROWS)
                pack[(c * GROUP + d) * BROWS + r, v * GROWS + row] = 1
    return unmix, pack, np.ascontiguousarray(pack.T), probs


UNMIX, PACK, UNPACK, PROBS = permutations()


def mm(a, b):
    return jnp.dot(a, b, preferred_element_type=F32)


def mm_t(a, b):
    return lax.dot_general(a, b, (((1,), (1,)), ((), ())), preferred_element_type=F32)


def iota(shape, dim):
    return lax.broadcasted_iota(jnp.int32, shape, dim)


def split_slot(ids):
    is_copy = (ids >= N).astype(jnp.int32)
    base = ids - N * is_copy
    target = jnp.where(ids >= N, jnp.bitwise_xor(base, N // 2), base)
    return target, is_copy * CAP


def places_in_lanes(ids_ref):
    ids = [ids_ref[k : k + 1, :] for k in range(2)]
    hot = [(iota((2 * N, TOK), 0) == v).astype(F32) for v in ids]
    before = (iota((TOK, TOK), 0) < iota((TOK, TOK), 1)).astype(F32).astype(BF16)
    count = mm((hot[0] + hot[1]).astype(BF16), before)
    out = []
    for k in range(2):
        rank = jnp.sum(count * hot[k], axis=0, keepdims=True).astype(jnp.int32)
        target, first = split_slot(ids[k])
        out.append((target, first + rank))
    return out


def places_in_rows(ids_ref):
    ids = [ids_ref[:, k : k + 1] for k in range(2)]
    hot = [(iota((TOK, 2 * N), 1) == v).astype(F32) for v in ids]
    before = (iota((TOK, TOK), 1) < iota((TOK, TOK), 0)).astype(F32).astype(BF16)
    count = mm(before, (hot[0] + hot[1]).astype(BF16))
    out = []
    for k in range(2):
        rank = jnp.sum(count * hot[k], axis=1, keepdims=True).astype(jnp.int32)
        target, first = split_slot(ids[k])
        out.append((target, first + rank))
    return out


def send_rows(ids_ref, weights, x_ref, out_ref):
    lanes = []
    for target, slot in places_in_lanes(ids_ref):
        at = target * SPAN + slot
        lanes.append(jnp.concatenate([at + s * PER for s in range(NSEG)], axis=1))
    stacked = jnp.concatenate([x_ref[:, s * SEG : (s + 1) * SEG] for s in range(NSEG)], axis=0)
    block = 384
    for c in range(N * SPAN // block):
        rows = iota((block, NSEG * TOK), 0) + c * block
        pick = jnp.where(
            rows == lanes[0], weights[0], jnp.where(rows == lanes[1], weights[1], 0.0)
        ).astype(BF16)
        out_ref[c * block : (c + 1) * block, :] = mm(pick, stacked).astype(BF16)


def send_tokens_kernel(ids_ref, x_ref, out_ref):
    send_rows(ids_ref, (1.0, 1.0), x_ref, out_ref)


def send_scaled_kernel(ids_ref, prob_ref, x_ref, out_ref):
    probs = [prob_ref[k : k + 1, :].astype(F32) for k in range(2)]
    weights = [jnp.concatenate([v] * NSEG, axis=1) for v in probs]
    send_rows(ids_ref, weights, x_ref, out_ref)


def unmix_rows(perm_ref, got_ref, rows_ref):
    perm = perm_ref[...]
    for g in range(NGROUP):
        part = mm(perm, got_ref[g * GROUP * SPAN : (g + 1) * GROUP * SPAN, :]).astype(BF16)
        for s in range(NSEG):
            rows_ref[s, g * GROWS : (g + 1) * GROWS, :] = part[s * GROWS : (s + 1) * GROWS]


def unmix_kernel(dp_ref, perm_ref, got_ref, rows, x0, x1, x2, x3):
    unmix_rows(perm_ref, got_ref, rows)
    for k, ref in enumerate((x0, x1, x2, x3)):
        which = lax.rem(dp_ref[0] + k, DP)
        ref[...] = rows[which].astype(F32).T.astype(BF16)


def scaled_kernel(dp_ref, perm_ref, got_ref, s0, s1, s2, s3, rows, sems):
    @pl.loop(0, NGROUP)
    def _(g):
        source = pl.ds(pl.multiple_of(g * GROUP * SPAN, 64), GROUP * SPAN)
        target = pl.ds(pl.multiple_of(g * GROWS, 16), GROWS)
        part = mm(perm_ref[...], got_ref[source, :]).astype(BF16)
        for s in range(NSEG):
            rows[s, target, :] = part[s * GROWS : (s + 1) * GROWS]

    copies = []
    for k, ref in enumerate((s1, s3, s2, s0)):
        which = lax.rem(dp_ref[0] + (1, 3, 2, 0)[k], DP)
        copies.append(pltpu.make_async_copy(rows.at[which], ref, sems.at[k]))
        copies[-1].start()
    for copy in copies:
        copy.wait()


def forward_kernel(
    rows, gate_hbm, up_hbm, gate_ref, up_ref, hidden_low, hidden_high, gate_w, up_w, sems
):
    half = FF // 2
    copies = []
    for i in range(2):
        at = pl.ds(i * half, half)
        for m, (source, target) in enumerate(((gate_hbm, gate_w), (up_hbm, up_w))):
            copies.append(
                pltpu.make_async_copy(source.at[:, at], target.at[:, at], sems.at[2 * i + m])
            )
            copies[-1].start()
    for i, out in enumerate((hidden_low, hidden_high)):
        at = slice(i * half, (i + 1) * half)
        copies[2 * i].wait()
        gate = sum(mm(rows[s], gate_w[s * SEG : (s + 1) * SEG, at]) for s in range(NSEG))
        copies[2 * i + 1].wait()
        up = sum(mm(rows[s], up_w[s * SEG : (s + 1) * SEG, at]) for s in range(NSEG))
        gate_ref[:, at] = gate.astype(BF16)
        up_ref[:, at] = up.astype(BF16)
        out[...] = (gate * jax.nn.sigmoid(gate) * up).T.astype(BF16)


def backward_kernel(
    perm_ref, got_ref, down_hbm, gate_hbm, up_hbm,
    back_ref, q_ref, gate_out, up_out, rows, down_w, gate_ref, up_ref, sems, loads,
):
    arriving = []
    for i in range(NFB):
        at = pl.ds(i * FB, FB)
        pairs = (
            (down_hbm.at[at], down_w.at[at]),
            (gate_hbm.at[:, at], gate_ref.at[:, at]),
            (up_hbm.at[:, at], up_ref.at[:, at]),
        )
        for m, (source, target) in enumerate(pairs):
            arriving.append(pltpu.make_async_copy(source, target, loads.at[3 * i + m]))
            arriving[-1].start()
    unmix_rows(perm_ref, got_ref, rows)
    copies = []
    total = jnp.zeros((ROWS, 1), F32)
    for i in range(NFB):
        at = slice(i * FB, (i + 1) * FB)
        for copy in arriving[3 * i : 3 * i + 3]:
            copy.wait()
        back_hidden = sum(mm_t(rows[s], down_w[at, s * SEG : (s + 1) * SEG]) for s in range(NSEG))
        gate = gate_ref[:, at].astype(F32)
        up = up_ref[:, at].astype(F32)
        sig = jax.nn.sigmoid(gate)
        activated = gate * sig
        hidden = (activated * up).astype(BF16).astype(F32)
        back_ref[0, :, at] = (back_hidden * up * sig * (1.0 + gate * (1.0 - sig))).astype(BF16)
        back_ref[1, :, at] = (back_hidden * activated).astype(BF16)
        total += jnp.sum(hidden * back_hidden, axis=1, keepdims=True)
        for m, ref in enumerate((gate_out, up_out)):
            part = pl.ds(i * FB, FB)
            copies.append(
                pltpu.make_async_copy(
                    back_ref.at[m, :, part], ref.at[:, part], sems.at[2 * i + m]
                )
            )
            copies[-1].start()
    q_ref[...] = jnp.broadcast_to(total, q_ref.shape)
    for copy in copies:
        copy.wait()


def send_back_kernel(pack_ref, probs_ref, back_ref, q_ref, gate_w, up_w, out_ref, rows, sent, sems):
    for i in range(NSEG):
        at = slice(i * SEG, (i + 1) * SEG)
        rows[:, at] = (mm_t(back_ref[0], gate_w[at, :]) + mm_t(back_ref[1], up_w[at, :])).astype(BF16)
    pack = pack_ref[...]
    height = GROUP * BROWS
    copies = []
    for g in range(NGROUP):
        lo, hi = g * GROWS, (g + 1) * GROWS
        stacked = jnp.concatenate(
            [
                jnp.concatenate(
                    [rows[lo:hi, (4 * u + v) * TILE : (4 * u + v + 1) * TILE] for u in range(NU)],
                    axis=1,
                )
                for v in range(4)
            ],
            axis=0,
        )
        part = mm(pack, stacked).astype(BF16)
        top = g * height
        for u in range(NU):
            for c in range(3):
                col = (3 * u + c) * TILE
                sent[top : top + height, col : col + TILE] = part[
                    c * height : (c + 1) * height, u * TILE : (u + 1) * TILE
                ]
        sent[top : top + height, 3 * NU * TILE :] = mm(
            probs_ref[...], q_ref[lo:hi, :].astype(BF16)
        ).astype(BF16)
        half = slice(top, top + height)
        copies.append(pltpu.make_async_copy(sent.at[half], out_ref.at[half], sems.at[g]))
        copies[-1].start()
    for copy in copies:
        copy.wait()


def load(sources, targets, sems):
    copies = [
        pltpu.make_async_copy(a, b, sems.at[i]) for i, (a, b) in enumerate(zip(sources, targets))
    ]
    for copy in copies:
        copy.start()
    return copies


def combine_kernel(
    ids_ref, ids_t_ref, prob_ref, perm_ref, got_hbm, tok_ref, gprob_ref, rows, got_ref, sems
):
    height = GROUP * BROWS
    blocks = [pl.ds(g * height, height) for g in range(NGROUP)]
    copies = load([got_hbm.at[b] for b in blocks], [got_ref.at[b] for b in blocks], sems)
    at = [target * PER + slot for target, slot in places_in_rows(ids_ref)]
    columns = iota((TOK, ROWS), 1)
    pick = jnp.where((columns == at[0]) | (columns == at[1]), 1.0, 0.0).astype(BF16)
    perm = perm_ref[...]
    for g in range(NGROUP):
        top = g * height
        copies[g].wait()
        stacked = jnp.concatenate(
            [
                jnp.concatenate(
                    [
                        got_ref[top : top + height, (3 * u + c) * TILE : (3 * u + c + 1) * TILE]
                        for u in range(NU)
                    ],
                    axis=1,
                )
                for c in range(3)
            ],
            axis=0,
        )
        part = mm(perm, stacked).astype(BF16)
        for u in range(NU):
            for v in range(4):
                col = (4 * u + v) * TILE
                rows[g * GROWS : (g + 1) * GROWS, col : col + TILE] = part[
                    v * GROWS : (v + 1) * GROWS, u * TILE : (u + 1) * TILE
                ]
    tok_ref[...] = mm(pick, rows[...]).astype(BF16)
    home = got_ref[:, 3 * NU * TILE :].astype(F32)
    line = iota((N * BROWS, TOK), 0)
    for k, (target, slot) in enumerate(places_in_lanes(ids_t_ref)):
        hit = jnp.where(line == target * BROWS + slot, home, 0.0)
        value = jnp.sum(hit, axis=0, keepdims=True)
        gprob_ref[k : k + 1, :] = (value / prob_ref[k : k + 1, :].astype(F32)).astype(BF16)


def down_grad_kernel(*refs):
    low, high, pieces = refs[:DP], refs[DP : 2 * DP], refs[2 * DP : 3 * DP]
    out_ref, lows, highs, cols, acc, sems = refs[3 * DP :]
    half = FF // 2
    order = (0, 1, 3, 2)
    copies = load(
        [r[k] for k in order for r in (pieces, low, high)],
        [r.at[k] for k in order for r in (cols, lows, highs)],
        sems,
    )
    for i, k in enumerate(order):
        for copy in copies[3 * i : 3 * i + 3]:
            copy.wait()
        for m, part in enumerate((lows, highs)):
            at = slice(m * half, (m + 1) * half)
            term = mm(part[k], cols[k])
            if i == 0:
                acc[at] = term
            elif i < DP - 1:
                acc[at] = acc[at] + term
            else:
                out_ref[at] = (acc[at] + term).astype(BF16)


def grad_first_kernel(*refs):
    acc, gates, ups, cols, sems = refs[9:]
    copies = load(
        [refs[3 * m + k] for k in range(3) for m in (2, 0, 1)],
        [r.at[k] for k in range(3) for r in (cols, gates, ups)],
        sems,
    )
    for k in range(3):
        for copy in copies[3 * k : 3 * k + 3]:
            copy.wait()
        for m, part in enumerate((gates, ups)):
            term = mm(cols[k], part[k])
            acc[m] = term if k == 0 else acc[m] + term


def grad_last_kernel(acc, gate_b, up_b, x2, gate_out, up_out, col, parts, sent, sems, out_sems):
    copies = load((x2, gate_b, up_b), (col, parts.at[0], parts.at[1]), sems)
    copies[0].wait()
    sends = []
    half = SEG // 2
    for m, out in enumerate((gate_out, up_out)):
        copies[1 + m].wait()
        for h in range(2):
            at = slice(h * half, (h + 1) * half)
            sent[m, at] = (acc[m, at] + mm(col[at], parts[m])).astype(BF16)
            rows = pl.ds(h * half, half)
            sends.append(
                pltpu.make_async_copy(sent.at[m, rows], out.at[rows], out_sems.at[2 * m + h])
            )
            sends[-1].start()
    for copy in sends:
        copy.wait()


def shape(dims, kind=BF16):
    return pltpu.HBM(dims, kind)


def near(dims, kind=BF16):
    return pltpu.VMEM(dims, kind)


def in_hbm(values):
    return pltpu.with_memory_space_constraint(values, pltpu.HBM)


def in_vmem(values):
    return pltpu.with_memory_space_constraint(values, pltpu.VMEM)


def call(kernel, out_shape, scratch=(), scalars=0, far=(), by_hand=(), flops=0):
    def run(*args):
        space = [pl.ANY if i in far else pltpu.VMEM for i in range(len(args))]
        space[:scalars] = [pltpu.SMEM] * scalars
        outs = [pl.ANY if i in by_hand else pltpu.VMEM for i in range(len(out_shape))]
        return pl.pallas_call(
            kernel,
            in_specs=[pl.BlockSpec(memory_space=v) for v in space],
            out_specs=[pl.BlockSpec(memory_space=v) for v in outs],
            out_shape=list(out_shape),
            scratch_shapes=list(scratch),
            compiler_params=pltpu.CompilerParams(vmem_limit_bytes=24 * 1024 * 1024),
            cost_estimate=pl.CostEstimate(flops=flops, bytes_accessed=8 << 20, transcendentals=0),
        )(*args)

    return run


def exchange(values):
    return lax.all_to_all(values, "expert", split_axis=0, concat_axis=0, tiled=True)


def shift(values, k):
    return lax.ppermute(values, "dp", [(i, (i + k) % DP) for i in range(DP)])


def spread(pieces):
    return [pieces[0]] + [shift(pieces[k], k) for k in range(1, DP)]


def around(low, high):
    low1 = shift(low, 1)
    high3 = shift(high, DP - 1)
    low3 = shift(low, DP - 1)
    high1 = shift(high, 1)
    low2 = shift(low1, 1)
    high2 = shift(high3, DP - 1)
    return (low, low1, low2, low3), (high, high1, high2, high3)


def body(tokens, cotangent, gate_probs, expert_ids, gate_weight, up_weight, down_weight):
    dp = lax.axis_index("dp").astype(jnp.int32).reshape(1)
    ids_t = expert_ids.T
    probs_t = gate_probs.T

    (send_x,) = call(send_tokens_kernel, [shape((N * SPAN, SEG))], flops=800 << 20)(
        in_hbm(ids_t), in_hbm(tokens)
    )
    got_x = exchange(send_x.reshape(N, SPAN, SEG)).reshape(N * SPAN, SEG)
    (send_c,) = call(send_scaled_kernel, [shape((N * SPAN, SEG))], flops=800 << 20)(
        ids_t, probs_t, cotangent
    )
    got_c = exchange(send_c.reshape(N, SPAN, SEG)).reshape(N * SPAN, SEG)

    unmix, pack, unpack, probs_perm = [jnp.asarray(v, BF16) for v in (UNMIX, PACK, UNPACK, PROBS)]

    rows, *x_pieces = call(
        unmix_kernel,
        [near((NSEG, ROWS, SEG))] + [shape((SEG, ROWS))] * DP,
        scalars=1, flops=300 << 20,
    )(dp, unmix, got_x)
    x_pieces = spread(x_pieces)
    gate, up, hidden_low, hidden_high = call(
        forward_kernel,
        [shape((ROWS, FF))] * 2 + [shape((FF // 2, ROWS))] * 2,
        scratch=[
            pltpu.VMEM((D, FF), BF16),
            pltpu.VMEM((D, FF), BF16),
            pltpu.SemaphoreType.DMA((4,)),
        ],
        far=(1, 2), flops=3000 << 20,
    )(in_vmem(rows), in_hbm(gate_weight[0]), in_hbm(up_weight[0]))
    h_low, h_high = around(hidden_low, hidden_high)

    back_near, q, back_gate, back_up = call(
        backward_kernel,
        [near((2, ROWS, FF)), near((ROWS, TILE), F32)]
        + [shape((ROWS, FF))] * 2,
        scratch=[
            pltpu.VMEM((NSEG, ROWS, SEG), BF16),
            pltpu.VMEM((FF, D), BF16),
            pltpu.VMEM((ROWS, FF), BF16),
            pltpu.VMEM((ROWS, FF), BF16),
            pltpu.SemaphoreType.DMA((2 * NFB,)),
            pltpu.SemaphoreType.DMA((3 * NFB,)),
        ],
        far=(2, 3, 4), by_hand=(2, 3), flops=2000 << 20,
    )(unmix, got_c, in_hbm(down_weight[0]), in_hbm(gate), in_hbm(up))
    b_gate, b_up = around(back_gate, back_up)
    s_pieces = call(
        scaled_kernel, [shape((ROWS, SEG))] * DP,
        scratch=[pltpu.VMEM((NSEG, ROWS, SEG), BF16), pltpu.SemaphoreType.DMA((DP,))],
        scalars=1, by_hand=(0, 1, 2, 3), flops=300 << 20,
    )(dp, unmix, got_c)
    s_pieces = spread(s_pieces)

    (send_b,) = call(
        send_back_kernel, [shape((N * BROWS, BCOLS))],
        scratch=[
            pltpu.VMEM((ROWS, D), BF16),
            pltpu.VMEM((N * BROWS, BCOLS), BF16),
            pltpu.SemaphoreType.DMA((NGROUP,)),
        ],
        by_hand=(0,), flops=3000 << 20,
    )(pack, probs_perm, in_vmem(back_near), in_vmem(q), in_vmem(gate_weight[0]), in_vmem(up_weight[0]))
    got_b = exchange(send_b.reshape(N, BROWS, BCOLS)).reshape(N * BROWS, BCOLS)

    (acc,) = call(
        grad_first_kernel, [near((2, SEG, FF), F32)],
        scratch=[
            pltpu.VMEM((3, ROWS, FF), BF16),
            pltpu.VMEM((3, ROWS, FF), BF16),
            pltpu.VMEM((3, SEG, ROWS), BF16),
            pltpu.SemaphoreType.DMA((9,)),
        ],
        far=range(9), flops=1800 << 20,
    )(*(b[k] for b in (b_gate, b_up, x_pieces) for k in (0, 1, 3)))
    (grad_down,) = call(
        down_grad_kernel, [shape((FF, SEG))],
        scratch=[
            pltpu.VMEM((DP, FF // 2, ROWS), BF16),
            pltpu.VMEM((DP, FF // 2, ROWS), BF16),
            pltpu.VMEM((DP, ROWS, SEG), BF16),
            pltpu.VMEM((FF, SEG), F32),
            pltpu.SemaphoreType.DMA((3 * DP,)),
        ],
        far=range(3 * DP), flops=1200 << 20,
    )(*h_low, *h_high, *s_pieces)
    grad_gate, grad_up = call(
        grad_last_kernel, [shape((SEG, FF))] * 2,
        scratch=[
            pltpu.VMEM((SEG, ROWS), BF16),
            pltpu.VMEM((2, ROWS, FF), BF16),
            pltpu.VMEM((2, SEG, FF), BF16),
            pltpu.SemaphoreType.DMA((3,)),
            pltpu.SemaphoreType.DMA((4,)),
        ],
        far=(1, 2, 3), by_hand=(0, 1), flops=600 << 20,
    )(in_vmem(acc), b_gate[2], b_up[2], x_pieces[2])
    grad_tokens, grad_probs = call(
        combine_kernel, [shape((TOK, D)), shape((2, TOK))],
        scratch=[
            pltpu.VMEM((ROWS, D), BF16),
            pltpu.VMEM((N * BROWS, BCOLS), BF16),
            pltpu.SemaphoreType.DMA((NGROUP,)),
        ],
        far=(4,), flops=1000 << 20,
    )(in_hbm(expert_ids), in_hbm(ids_t), in_hbm(probs_t), in_hbm(unpack), got_b)
    return grad_tokens, grad_probs.T, grad_gate[None], grad_up[None], grad_down[None]


def solution(mesh):
    in_specs = (
        P(("dp", "expert"), None),
        P(("dp", "expert"), None),
        P(("dp", "expert"), None),
        P(("dp", "expert"), None),
        P("expert", None, None),
        P("expert", None, None),
        P("expert", None, None),
    )
    out_specs = (
        P(("dp", "expert"), None),
        P(("dp", "expert"), None),
        P("expert", "dp", None),
        P("expert", "dp", None),
        P("expert", None, "dp"),
    )

    return jax.shard_map(body, mesh=mesh, in_specs=in_specs, out_specs=out_specs, check_vma=False)
```

```python
import jax
import jax.numpy as jnp
import numpy as np
from jax import lax
from jax.experimental import pallas as pl
from jax.experimental.pallas import tpu as pltpu
from jax.sharding import PartitionSpec as P


F32 = jnp.float32
BF16 = jnp.bfloat16
N = 64
CAP = 3
PER = 2 * CAP
ROWS = N * PER
D = 2048
FF = 768
TOK = 128
DP = 4
SEG = 512
NSEG = D // SEG
SPAN = NSEG * PER
TILE = 128
NU = D // (4 * TILE)
BROWS = 8
BCOLS = (3 * NU + 1) * TILE
GROUP = 8
GROWS = GROUP * PER
NGROUP = N // GROUP
FB = 256
NFB = FF // FB


def permutations():
    unmix = np.zeros((NSEG * GROWS, GROUP * SPAN), np.float32)
    pack = np.zeros((3 * GROUP * BROWS, 4 * GROWS), np.float32)
    probs = np.zeros((GROUP * BROWS, GROWS), np.float32)
    for d in range(GROUP):
        for j in range(PER):
            row = d * PER + j
            probs[d * BROWS + j, row] = 1
            for s in range(NSEG):
                unmix[s * GROWS + row, d * SPAN + s * PER + j] = 1
            for v in range(4):
                c, r = divmod(v * PER + j, BROWS)
                pack[(c * GROUP + d) * BROWS + r, v * GROWS + row] = 1
    return unmix, pack, probs


UNMIX, PACK, PROBS = permutations()


def mm(a, b):
    return jnp.dot(a, b, preferred_element_type=F32)


def mm_t(a, b):
    return lax.dot_general(a, b, (((1,), (1,)), ((), ())), preferred_element_type=F32)


def iota(shape, dim):
    return lax.broadcasted_iota(jnp.int32, shape, dim)


def split_slot(ids):
    is_copy = (ids >= N).astype(jnp.int32)
    base = ids - N * is_copy
    target = jnp.where(ids >= N, jnp.bitwise_xor(base, N // 2), base)
    return target, is_copy * CAP


def places_in_lanes(ids_ref):
    ids = [ids_ref[k : k + 1, :] for k in range(2)]
    hot = [(iota((2 * N, TOK), 0) == v).astype(F32) for v in ids]
    before = (iota((TOK, TOK), 0) < iota((TOK, TOK), 1)).astype(F32).astype(BF16)
    count = mm((hot[0] + hot[1]).astype(BF16), before)
    out = []
    for k in range(2):
        rank = jnp.sum(count * hot[k], axis=0, keepdims=True).astype(jnp.int32)
        target, first = split_slot(ids[k])
        out.append((target, first + rank))
    return out


def send_rows(ids_ref, weights, x_ref, out_ref):
    lanes = []
    for target, slot in places_in_lanes(ids_ref):
        at = target * SPAN + slot
        lanes.append(jnp.concatenate([at + s * PER for s in range(NSEG)], axis=1))
    stacked = jnp.concatenate([x_ref[:, s * SEG : (s + 1) * SEG] for s in range(NSEG)], axis=0)
    block = 384
    for c in range(N * SPAN // block):
        rows = iota((block, NSEG * TOK), 0) + c * block
        pick = jnp.where(
            rows == lanes[0], weights[0], jnp.where(rows == lanes[1], weights[1], 0.0)
        ).astype(BF16)
        out_ref[c * block : (c + 1) * block, :] = mm(pick, stacked).astype(BF16)


def send_tokens_kernel(ids_ref, x_ref, out_ref):
    send_rows(ids_ref, (1.0, 1.0), x_ref, out_ref)


def send_scaled_kernel(ids_ref, prob_ref, x_ref, out_ref):
    probs = [prob_ref[k : k + 1, :].astype(F32) for k in range(2)]
    weights = [jnp.concatenate([v] * NSEG, axis=1) for v in probs]
    send_rows(ids_ref, weights, x_ref, out_ref)


def unmix_rows(perm_ref, got_ref, rows_ref):
    perm = perm_ref[...]
    for g in range(NGROUP):
        part = mm(perm, got_ref[g * GROUP * SPAN : (g + 1) * GROUP * SPAN, :]).astype(BF16)
        for s in range(NSEG):
            rows_ref[s, g * GROWS : (g + 1) * GROWS, :] = part[s * GROWS : (s + 1) * GROWS]


def unmix_kernel(dp_ref, perm_ref, got_ref, rows, x0, x1, x2, x3):
    unmix_rows(perm_ref, got_ref, rows)
    for k, ref in enumerate((x0, x1, x2, x3)):
        which = lax.rem(dp_ref[0] + k, DP)
        ref[...] = rows[which].astype(F32).T.astype(BF16)


def scaled_kernel(dp_ref, perm_ref, got_ref, s0, s1, s2, s3, rows, sems):
    @pl.loop(0, NGROUP)
    def _(g):
        source = pl.ds(pl.multiple_of(g * GROUP * SPAN, 64), GROUP * SPAN)
        target = pl.ds(pl.multiple_of(g * GROWS, 16), GROWS)
        part = mm(perm_ref[...], got_ref[source, :]).astype(BF16)
        for s in range(NSEG):
            rows[s, target, :] = part[s * GROWS : (s + 1) * GROWS]

    copies = []
    for k, ref in enumerate((s1, s3, s2, s0)):
        which = lax.rem(dp_ref[0] + (1, 3, 2, 0)[k], DP)
        copies.append(pltpu.make_async_copy(rows.at[which], ref, sems.at[k]))
        copies[-1].start()
    for copy in copies:
        copy.wait()


def forward_kernel(
    rows, gate_hbm, up_hbm, gate_ref, up_ref, hidden_low, hidden_high, gate_w, up_w, sems
):
    half = FF // 2
    copies = []
    for i in range(2):
        at = pl.ds(i * half, half)
        for m, (source, target) in enumerate(((gate_hbm, gate_w), (up_hbm, up_w))):
            copies.append(
                pltpu.make_async_copy(source.at[:, at], target.at[:, at], sems.at[2 * i + m])
            )
            copies[-1].start()
    for i, out in enumerate((hidden_low, hidden_high)):
        at = slice(i * half, (i + 1) * half)
        copies[2 * i].wait()
        gate = sum(mm(rows[s], gate_w[s * SEG : (s + 1) * SEG, at]) for s in range(NSEG))
        copies[2 * i + 1].wait()
        up = sum(mm(rows[s], up_w[s * SEG : (s + 1) * SEG, at]) for s in range(NSEG))
        gate_ref[:, at] = gate.astype(BF16)
        up_ref[:, at] = up.astype(BF16)
        out[...] = (gate * jax.nn.sigmoid(gate) * up).T.astype(BF16)


def backward_kernel(
    perm_ref, got_ref, down_hbm, gate_hbm, up_hbm,
    back_ref, q_ref, gate_out, up_out, rows, down_w, gate_ref, up_ref, sems, loads,
):
    arriving = []
    for i in range(NFB):
        at = pl.ds(i * FB, FB)
        pairs = (
            (down_hbm.at[at], down_w.at[at]),
            (gate_hbm.at[:, at], gate_ref.at[:, at]),
            (up_hbm.at[:, at], up_ref.at[:, at]),
        )
        for m, (source, target) in enumerate(pairs):
            arriving.append(pltpu.make_async_copy(source, target, loads.at[3 * i + m]))
            arriving[-1].start()
    unmix_rows(perm_ref, got_ref, rows)
    copies = []
    total = jnp.zeros((ROWS, 1), F32)
    for i in range(NFB):
        at = slice(i * FB, (i + 1) * FB)
        for copy in arriving[3 * i : 3 * i + 3]:
            copy.wait()
        back_hidden = sum(mm_t(rows[s], down_w[at, s * SEG : (s + 1) * SEG]) for s in range(NSEG))
        gate = gate_ref[:, at].astype(F32)
        up = up_ref[:, at].astype(F32)
        sig = jax.nn.sigmoid(gate)
        activated = gate * sig
        hidden = (activated * up).astype(BF16).astype(F32)
        back_ref[0, :, at] = (back_hidden * up * sig * (1.0 + gate * (1.0 - sig))).astype(BF16)
        back_ref[1, :, at] = (back_hidden * activated).astype(BF16)
        total += jnp.sum(hidden * back_hidden, axis=1, keepdims=True)
        for m, ref in enumerate((gate_out, up_out)):
            part = pl.ds(i * FB, FB)
            copies.append(
                pltpu.make_async_copy(
                    back_ref.at[m, :, part], ref.at[:, part], sems.at[2 * i + m]
                )
            )
            copies[-1].start()
    q_ref[...] = jnp.broadcast_to(total, q_ref.shape)
    for copy in copies:
        copy.wait()


def send_back_kernel(pack_ref, probs_ref, back_ref, q_ref, gate_w, up_w, out_ref, rows, sent, sems):
    for i in range(NSEG):
        at = slice(i * SEG, (i + 1) * SEG)
        rows[:, at] = (mm_t(back_ref[0], gate_w[at, :]) + mm_t(back_ref[1], up_w[at, :])).astype(BF16)
    pack = pack_ref[...]
    height = GROUP * BROWS
    copies = []
    for g in range(NGROUP):
        lo, hi = g * GROWS, (g + 1) * GROWS
        stacked = jnp.concatenate(
            [
                jnp.concatenate(
                    [rows[lo:hi, (4 * u + v) * TILE : (4 * u + v + 1) * TILE] for u in range(NU)],
                    axis=1,
                )
                for v in range(4)
            ],
            axis=0,
        )
        part = mm(pack, stacked).astype(BF16)
        top = g * height
        for u in range(NU):
            for c in range(3):
                col = (3 * u + c) * TILE
                sent[top : top + height, col : col + TILE] = part[
                    c * height : (c + 1) * height, u * TILE : (u + 1) * TILE
                ]
        sent[top : top + height, 3 * NU * TILE :] = mm(
            probs_ref[...], q_ref[lo:hi, :].astype(BF16)
        ).astype(BF16)
        half = slice(top, top + height)
        copies.append(pltpu.make_async_copy(sent.at[half], out_ref.at[half], sems.at[g]))
        copies[-1].start()
    for copy in copies:
        copy.wait()


def load(sources, targets, sems):
    copies = [
        pltpu.make_async_copy(a, b, sems.at[i]) for i, (a, b) in enumerate(zip(sources, targets))
    ]
    for copy in copies:
        copy.start()
    return copies


def unpack_matrix():
    size = 4 * GROWS

    def sixth(v):
        return lax.shift_right_logical(v * 43691, 18)

    a = iota((size, 1), 0)
    owner = sixth(a)
    piece = lax.shift_right_logical(owner, 3) * PER + a - owner * PER
    b = iota((1, size), 1)
    line = lax.shift_right_logical(b, 3)
    slot = lax.shift_right_logical(line, 3) * BROWS + (b & 7)
    hit = (piece == slot) & ((owner & 7) == (line & 7))
    return jnp.where(hit, 1.0, 0.0).astype(BF16)


def combine_kernel(ids_t_ref, prob_ref, got_ref, tok_ref, gprob_ref, rows):
    height = GROUP * BROWS
    places = places_in_lanes(ids_t_ref)
    at = [target * PER + slot for target, slot in places]
    lines = iota((ROWS, TOK), 0)
    pick = jnp.where((lines == at[0]) | (lines == at[1]), 1.0, 0.0).T.astype(BF16)
    perm = unpack_matrix()
    for g in range(NGROUP):
        top = g * height
        stacked = jnp.concatenate(
            [
                jnp.concatenate(
                    [
                        got_ref[top : top + height, (3 * u + c) * TILE : (3 * u + c + 1) * TILE]
                        for u in range(NU)
                    ],
                    axis=1,
                )
                for c in range(3)
            ],
            axis=0,
        )
        part = mm(perm, stacked).astype(BF16)
        for u in range(NU):
            for v in range(4):
                col = (4 * u + v) * TILE
                rows[g * GROWS : (g + 1) * GROWS, col : col + TILE] = part[
                    v * GROWS : (v + 1) * GROWS, u * TILE : (u + 1) * TILE
                ]
    tok_ref[...] = mm(pick, rows[...]).astype(BF16)
    home = got_ref[:, 3 * NU * TILE :].astype(F32)
    line = iota((N * BROWS, TOK), 0)
    for k, (target, slot) in enumerate(places):
        hit = jnp.where(line == target * BROWS + slot, home, 0.0)
        value = jnp.sum(hit, axis=0, keepdims=True)
        gprob_ref[k : k + 1, :] = (value / prob_ref[k : k + 1, :].astype(F32)).astype(BF16)


def down_grad_kernel(*refs):
    low, high, pieces = refs[:DP], refs[DP : 2 * DP], refs[2 * DP : 3 * DP]
    out_ref, lows, highs, cols, acc, sems = refs[3 * DP :]
    half = FF // 2
    order = (0, 1, 3, 2)
    copies = load(
        [r[k] for k in order for r in (pieces, low, high)],
        [r.at[k] for k in order for r in (cols, lows, highs)],
        sems,
    )
    for i, k in enumerate(order):
        for copy in copies[3 * i : 3 * i + 3]:
            copy.wait()
        for m, part in enumerate((lows, highs)):
            at = slice(m * half, (m + 1) * half)
            term = mm(part[k], cols[k])
            if i == 0:
                acc[at] = term
            elif i < DP - 1:
                acc[at] = acc[at] + term
            else:
                out_ref[at] = (acc[at] + term).astype(BF16)


def grad_first_kernel(*refs):
    out, gates, ups, cols, acc, sems = refs[9:]
    copies = load(
        [refs[3 * m + k] for k in range(3) for m in (2, 0, 1)],
        [r.at[k] for k in range(3) for r in (cols, gates, ups)],
        sems,
    )
    for k in range(3):
        for copy in copies[3 * k : 3 * k + 3]:
            copy.wait()
        for m, part in enumerate((gates, ups)):
            term = mm(cols[k], part[k])
            if k == 0:
                acc[m] = term
            elif k == 1:
                acc[m] = acc[m] + term
            else:
                out[m] = (acc[m] + term).astype(BF16)


def grad_last_kernel(acc, gate_b, up_b, x2, gate_out, up_out, col, parts, sent, sems, out_sems):
    copies = load((x2, gate_b, up_b), (col, parts.at[0], parts.at[1]), sems)
    copies[0].wait()
    sends = []
    half = SEG // 2
    for m, out in enumerate((gate_out, up_out)):
        copies[1 + m].wait()
        for h in range(2):
            at = slice(h * half, (h + 1) * half)
            sent[m, at] = (acc[m, at].astype(F32) + mm(col[at], parts[m])).astype(BF16)
            rows = pl.ds(h * half, half)
            sends.append(
                pltpu.make_async_copy(sent.at[m, rows], out.at[rows], out_sems.at[2 * m + h])
            )
            sends[-1].start()
    for copy in sends:
        copy.wait()


def shape(dims, kind=BF16):
    return pltpu.HBM(dims, kind)


def near(dims, kind=BF16):
    return pltpu.VMEM(dims, kind)


def in_hbm(values):
    return pltpu.with_memory_space_constraint(values, pltpu.HBM)


def in_vmem(values):
    return pltpu.with_memory_space_constraint(values, pltpu.VMEM)


def call(kernel, out_shape, scratch=(), scalars=0, far=(), by_hand=(), flops=0):
    def run(*args):
        space = [pl.ANY if i in far else pltpu.VMEM for i in range(len(args))]
        space[:scalars] = [pltpu.SMEM] * scalars
        outs = [pl.ANY if i in by_hand else pltpu.VMEM for i in range(len(out_shape))]
        return pl.pallas_call(
            kernel,
            in_specs=[pl.BlockSpec(memory_space=v) for v in space],
            out_specs=[pl.BlockSpec(memory_space=v) for v in outs],
            out_shape=list(out_shape),
            scratch_shapes=list(scratch),
            compiler_params=pltpu.CompilerParams(vmem_limit_bytes=24 * 1024 * 1024),
            cost_estimate=pl.CostEstimate(flops=flops, bytes_accessed=8 << 20, transcendentals=0),
        )(*args)

    return run


def exchange(values):
    return lax.all_to_all(values, "expert", split_axis=0, concat_axis=0, tiled=True)


def shift(values, k):
    return lax.ppermute(values, "dp", [(i, (i + k) % DP) for i in range(DP)])


def spread(pieces):
    return [pieces[0]] + [shift(pieces[k], k) for k in range(1, DP)]


def around(low, high):
    low1 = shift(low, 1)
    high3 = shift(high, DP - 1)
    low3 = shift(low, DP - 1)
    high1 = shift(high, 1)
    low2 = shift(low1, 1)
    high2 = shift(high3, DP - 1)
    return (low, low1, low2, low3), (high, high1, high2, high3)


def body(tokens, cotangent, gate_probs, expert_ids, gate_weight, up_weight, down_weight):
    dp = lax.axis_index("dp").astype(jnp.int32).reshape(1)
    ids_t = expert_ids.T
    probs_t = gate_probs.T

    (send_x,) = call(send_tokens_kernel, [shape((N * SPAN, SEG))], flops=800 << 20)(
        in_hbm(ids_t), in_hbm(tokens)
    )
    got_x = exchange(send_x.reshape(N, SPAN, SEG)).reshape(N * SPAN, SEG)
    (send_c,) = call(send_scaled_kernel, [shape((N * SPAN, SEG))], flops=800 << 20)(
        ids_t, probs_t, cotangent
    )
    got_c = exchange(send_c.reshape(N, SPAN, SEG)).reshape(N * SPAN, SEG)

    unmix, pack, probs_perm = [jnp.asarray(v, BF16) for v in (UNMIX, PACK, PROBS)]

    rows, *x_pieces = call(
        unmix_kernel,
        [near((NSEG, ROWS, SEG))] + [shape((SEG, ROWS))] * DP,
        scalars=1, flops=300 << 20,
    )(dp, unmix, got_x)
    x_pieces = spread(x_pieces)
    gate, up, hidden_low, hidden_high = call(
        forward_kernel,
        [shape((ROWS, FF))] * 2 + [shape((FF // 2, ROWS))] * 2,
        scratch=[
            pltpu.VMEM((D, FF), BF16),
            pltpu.VMEM((D, FF), BF16),
            pltpu.SemaphoreType.DMA((4,)),
        ],
        far=(1, 2), flops=3000 << 20,
    )(in_vmem(rows), in_hbm(gate_weight[0]), in_hbm(up_weight[0]))
    h_low, h_high = around(hidden_low, hidden_high)

    back_near, q, back_gate, back_up = call(
        backward_kernel,
        [near((2, ROWS, FF)), near((ROWS, TILE), F32)]
        + [shape((ROWS, FF))] * 2,
        scratch=[
            pltpu.VMEM((NSEG, ROWS, SEG), BF16),
            pltpu.VMEM((FF, D), BF16),
            pltpu.VMEM((ROWS, FF), BF16),
            pltpu.VMEM((ROWS, FF), BF16),
            pltpu.SemaphoreType.DMA((2 * NFB,)),
            pltpu.SemaphoreType.DMA((3 * NFB,)),
        ],
        far=(2, 3, 4), by_hand=(2, 3), flops=2000 << 20,
    )(unmix, got_c, in_hbm(down_weight[0]), in_hbm(gate), in_hbm(up))
    b_gate, b_up = around(back_gate, back_up)
    s_pieces = call(
        scaled_kernel, [shape((ROWS, SEG))] * DP,
        scratch=[pltpu.VMEM((NSEG, ROWS, SEG), BF16), pltpu.SemaphoreType.DMA((DP,))],
        scalars=1, by_hand=(0, 1, 2, 3), flops=300 << 20,
    )(dp, unmix, got_c)
    s_pieces = spread(s_pieces)

    (send_b,) = call(
        send_back_kernel, [shape((N * BROWS, BCOLS))],
        scratch=[
            pltpu.VMEM((ROWS, D), BF16),
            pltpu.VMEM((N * BROWS, BCOLS), BF16),
            pltpu.SemaphoreType.DMA((NGROUP,)),
        ],
        by_hand=(0,), flops=3000 << 20,
    )(pack, probs_perm, in_vmem(back_near), in_vmem(q), in_vmem(gate_weight[0]), in_vmem(up_weight[0]))
    got_b = exchange(send_b.reshape(N, BROWS, BCOLS)).reshape(N * BROWS, BCOLS)

    (acc,) = call(
        grad_first_kernel, [near((2, SEG, FF))],
        scratch=[
            pltpu.VMEM((3, ROWS, FF), BF16),
            pltpu.VMEM((3, ROWS, FF), BF16),
            pltpu.VMEM((3, SEG, ROWS), BF16),
            pltpu.VMEM((2, SEG, FF), F32),
            pltpu.SemaphoreType.DMA((9,)),
        ],
        far=range(9), flops=1800 << 20,
    )(*(b[k] for b in (b_gate, b_up, x_pieces) for k in (0, 1, 3)))
    (grad_down,) = call(
        down_grad_kernel, [shape((FF, SEG))],
        scratch=[
            pltpu.VMEM((DP, FF // 2, ROWS), BF16),
            pltpu.VMEM((DP, FF // 2, ROWS), BF16),
            pltpu.VMEM((DP, ROWS, SEG), BF16),
            pltpu.VMEM((FF, SEG), F32),
            pltpu.SemaphoreType.DMA((3 * DP,)),
        ],
        far=range(3 * DP), flops=1200 << 20,
    )(*h_low, *h_high, *s_pieces)
    grad_gate, grad_up = call(
        grad_last_kernel, [shape((SEG, FF))] * 2,
        scratch=[
            pltpu.VMEM((SEG, ROWS), BF16),
            pltpu.VMEM((2, ROWS, FF), BF16),
            pltpu.VMEM((2, SEG, FF), BF16),
            pltpu.SemaphoreType.DMA((3,)),
            pltpu.SemaphoreType.DMA((4,)),
        ],
        far=(1, 2, 3), by_hand=(0, 1), flops=600 << 20,
    )(in_vmem(acc), b_gate[2], b_up[2], x_pieces[2])
    grad_tokens, grad_probs = call(
        combine_kernel, [shape((TOK, D)), shape((2, TOK))],
        scratch=[pltpu.VMEM((ROWS, D), BF16)], flops=1000 << 20,
    )(ids_t, probs_t, got_b)
    return grad_tokens, grad_probs.T, grad_gate[None], grad_up[None], grad_down[None]


def solution(mesh):
    in_specs = (
        P(("dp", "expert"), None),
        P(("dp", "expert"), None),
        P(("dp", "expert"), None),
        P(("dp", "expert"), None),
        P("expert", None, None),
        P("expert", None, None),
        P("expert", None, None),
    )
    out_specs = (
        P(("dp", "expert"), None),
        P(("dp", "expert"), None),
        P("expert", "dp", None),
        P("expert", "dp", None),
        P("expert", None, "dp"),
    )

    return jax.shard_map(body, mesh=mesh, in_specs=in_specs, out_specs=out_specs, check_vma=False)
```
